256 devices in a mesh: row: 32 (over y, x, core), col: 8 (over z).
Axes of the slice: x: 4, y: 4, z: 8, core: 2. Of those that a mesh axis runs over, the one named last changes fastest.
Arguments:
- values: float32 [32, 8, 68, 128, 128], P('row', 'col'), as said below
- block_ids: int32 [32, 8, 68, 2], P('row', 'col'), may hold values from -1 to 255, as said below
- coupled_rows: int32 [32, 4], replicated, may hold values from 0 to 255, as said below
Outputs:
- factored: float32 [32, 8, 68, 128, 128], P('row', 'col')
The draws below stay inside these ranges and needn't reach their ends.
Inputs may be any that keep to these rules, and one draw needn't show every extreme that they name: `coupled_rows`: row r holds 4 distinct block rows in increasing order, each equal to r modulo 32; every block row below 4 is among them. `block_ids`: the slots of device (r, c), in an order drawn from the seed, name each block (i, j) with i in row r of coupled_rows, j in a row r2 of coupled_rows with r2 equal to c modulo 8, and j <= i; and each diagonal block (i, i) of a block row i equal to r modulo 32 and to c modulo 8 that is not coupled; every other slot holds (-1, -1). No block is named twice. `values`: every stored diagonal block is symmetric, and the blocks of A in block rows and block columns below 4 form a symmetric positive definite matrix.
All inputs are finite; a program needn't handle non-finite values.
Results may differ from the reference program's by a relative error of at most 0.0003.
Values sent between devices are 32-bit elements; how exact they have to be, the bound alone decides.
A program may use at most 128 MiB of HBM per device.

```python
import jax
import jax.numpy as jnp
from jax import lax

BLK = 128
BROWS = 8
SR = 4
PANELS = 4
N_ROW = 32
N_COL = 8


def layout(key):
    base = jax.random.fold_in(key, 11)
    row_keys = jax.random.split(jax.random.fold_in(base, 1), N_ROW)
    local_rows = jnp.arange(BROWS, dtype=jnp.int32)

    def shuffle_row(row_key, row_index):
        shuffled = jax.random.permutation(row_key, BROWS).astype(jnp.int32)
        zero_at = jnp.sum(jnp.where(shuffled == 0, local_rows, 0))
        forced = (row_index < PANELS) & (zero_at >= SR)
        last_row = shuffled[SR - 1]
        moved = jnp.where(forced & (local_rows == SR - 1), 0, shuffled)
        return jnp.where(forced & (local_rows == zero_at), last_row, moved)
    orders = jax.vmap(shuffle_row)(row_keys, jnp.arange(N_ROW, dtype=jnp.int32))
    row_index = jnp.arange(N_ROW, dtype=jnp.int32)[:, None]
    coupled = jnp.sort(orders[:, :SR], axis=1) * N_ROW + row_index
    spare = orders[:, SR:] * N_ROW + row_index
    groups = N_ROW // N_COL
    col_sets = jnp.transpose(coupled.reshape(groups, N_COL, SR), (1, 0, 2)).reshape(N_COL, groups * SR)
    left_ids = jnp.broadcast_to(coupled[:, None, :, None], (N_ROW, N_COL, SR, groups * SR))
    right_ids = jnp.broadcast_to(col_sets[None, :, None, :], (N_ROW, N_COL, SR, groups * SR))
    lower = right_ids <= left_ids
    pair_rows = jnp.where(lower, left_ids, -1).reshape(N_ROW, N_COL, SR * groups * SR)
    pair_cols = jnp.where(lower, right_ids, -1).reshape(N_ROW, N_COL, SR * groups * SR)
    holds = jnp.arange(N_ROW, dtype=jnp.int32)[:, None] % N_COL == jnp.arange(N_COL, dtype=jnp.int32)[None, :]
    spare_ids = jnp.where(holds[:, :, None], spare[:, None, :], -1)
    all_rows = jnp.concatenate([pair_rows, spare_ids], axis=2)
    all_cols = jnp.concatenate([pair_cols, spare_ids], axis=2)
    slot_count = all_rows.shape[2]
    slot_keys = jax.random.split(jax.random.fold_in(base, 2), N_ROW * N_COL)

    def slot_order(slot_key):
        return jax.random.permutation(slot_key, slot_count).astype(jnp.int32)
    reorder = jax.vmap(slot_order)(slot_keys).reshape(N_ROW, N_COL, slot_count)
    all_rows = jnp.take_along_axis(all_rows, reorder, axis=2)
    all_cols = jnp.take_along_axis(all_cols, reorder, axis=2)
    block_list = jnp.stack([all_rows, all_cols], axis=-1).astype(jnp.int32)
    return (coupled.astype(jnp.int32), block_list)


def draw_coupled_rows(key, part):
    coupled, block_list = layout(key)
    return coupled


def draw_block_ids(key, part):
    coupled, block_list = layout(key)
    return block_list


def draw_values(key, part):
    coupled, block_list = layout(key)
    key_lead, key_diagonal, key_blocks, key_filler = jax.random.split(jax.random.fold_in(key, 23), 4)
    total_rows = BROWS * N_ROW
    lead_order = PANELS * BLK
    panel_scale = 0.3
    lead_ints = jax.random.randint(key_lead, (lead_order, lead_order), -3, 4)
    lead_scale = 1.0 / (4.0 * lead_order)
    diagonal = jax.random.uniform(key_diagonal, (total_rows, BLK), jnp.float32, 0.25, 1.0)
    lead_float = lead_ints.astype(jnp.float32)
    leading = jnp.dot(lead_float, lead_float.T, precision=lax.Precision.HIGHEST) * lead_scale
    leading = jnp.transpose(leading.reshape(PANELS, BLK, PANELS, BLK), (0, 2, 1, 3))
    identity = jnp.eye(BLK, dtype=jnp.float32)
    slot_count = block_list.shape[2]
    filler = jax.random.normal(key_filler, (N_ROW * N_COL, slot_count, BLK, BLK), jnp.float32)
    flat_list = block_list.reshape(N_ROW * N_COL, slot_count, 2)

    def block_noise(block_row, block_col):
        block_key = jax.random.fold_in(jax.random.fold_in(key_blocks, block_row), block_col)
        fresh = jax.random.normal(block_key, (BLK, BLK), jnp.float32)
        return fresh

    def device_blocks(carried):
        device_ids, device_filler = carried
        rows_here = jnp.maximum(device_ids[:, 0], 0)
        cols_here = jnp.maximum(device_ids[:, 1], 0)
        noise = jax.vmap(block_noise)(rows_here, cols_here)
        same = (rows_here == cols_here)[:, None, None]
        symmetric = jnp.where(same, (noise + jnp.swapaxes(noise, 1, 2)) * 0.70710678, noise)
        diagonal_add = jnp.where(same, diagonal[rows_here][:, :, None] * identity[None], 0.0)
        lead_rows = jnp.minimum(rows_here, PANELS - 1)
        lead_cols = jnp.minimum(cols_here, PANELS - 1)
        lead_block = leading[lead_rows, lead_cols] + diagonal_add
        panel_block = panel_scale * noise
        trail_block = symmetric + diagonal_add
        is_lead = (rows_here < PANELS)[:, None, None]
        is_panel = (cols_here < PANELS)[:, None, None]
        stored = jnp.where(is_lead, lead_block, jnp.where(is_panel, panel_block, trail_block))
        return jnp.where((device_ids[:, 0] >= 0)[:, None, None], stored, device_filler)
    result = lax.map(device_blocks, (flat_list, filler))
    return result.reshape(N_ROW, N_COL, slot_count, BLK, BLK)


def setup_inputs(seed: int = 0) -> dict:
    seeds = jax.random.split(jax.random.key(seed), 4)
    return {
        "values": draw_values(jax.random.fold_in(seeds[3], 71), 0),
        "block_ids": draw_block_ids(jax.random.fold_in(seeds[3], 71), 0),
        "coupled_rows": draw_coupled_rows(jax.random.fold_in(seeds[3], 71), 0),
    }


exact_precision = lax.Precision.HIGHEST

def locate(wanted, known_rows):
    matched = wanted[:, None] == known_rows[None, :]
    places = jnp.arange(known_rows.shape[0], dtype=jnp.int32)
    found_at = jnp.sum(jnp.where(matched, places[None, :], 0), axis=1).astype(jnp.int32)
    return (found_at, jnp.any(matched, axis=1))

def reference(values, block_ids, coupled_rows):
    device_count = values.shape[0] * values.shape[1]
    slot_count = values.shape[2]
    block_size = values.shape[-1]
    state = values.reshape(device_count, slot_count, block_size, block_size)
    flat_ids = block_ids.reshape(device_count, slot_count, 2).astype(jnp.int32)
    row_ids = flat_ids[:, :, 0]
    col_ids = flat_ids[:, :, 1]
    members = coupled_rows.reshape(-1).astype(jnp.int32)
    member_count = members.shape[0]
    member_places = jnp.arange(member_count, dtype=jnp.int32)
    row_flat, row_found = locate(row_ids.reshape(-1), members)
    col_flat, col_found = locate(col_ids.reshape(-1), members)
    coupled_flat = row_found & col_found
    row_place = row_flat.reshape(device_count, slot_count)
    col_place = col_flat.reshape(device_count, slot_count)
    coupled = coupled_flat.reshape(device_count, slot_count)
    slot_numbers = jnp.arange(device_count * slot_count, dtype=jnp.int32)
    identity = jnp.eye(block_size, dtype=jnp.float32)
    for column in range(PANELS):
        flat_state = state.reshape(device_count * slot_count, block_size, block_size)
        in_column = coupled_flat & (col_ids.reshape(-1) == column)
        chosen = in_column[:, None] & (row_flat[:, None] == member_places[None, :])
        slot_of = jnp.sum(jnp.where(chosen, slot_numbers[:, None], 0), axis=0).astype(jnp.int32)
        present = jnp.any(chosen, axis=0)
        raw_panel = jnp.where(present[:, None, None], flat_state[slot_of], 0.0)
        pivot_at = jnp.argmax((members == column).astype(jnp.int32))
        pivot_factor = jnp.linalg.cholesky(raw_panel[pivot_at])
        inverse = jax.scipy.linalg.solve_triangular(pivot_factor, identity, lower=True)
        scaled = jnp.einsum('mab,cb->mac', raw_panel, inverse, precision=exact_precision)
        panel_blocks = jnp.where((members > column)[:, None, None], scaled, jnp.where((members == column)[:, None, None], pivot_factor[None], 0.0))

        def update_device(carried):
            device_values, device_rows, device_cols, device_col_ids, device_coupled = carried
            left_block = panel_blocks[device_rows]
            right_block = panel_blocks[device_cols]
            product = jnp.einsum('sab,scb->sac', left_block, right_block, precision=exact_precision)
            active = device_coupled & (device_col_ids > column)
            updated = device_values - jnp.where(active[:, None, None], product, 0.0)
            replace = device_coupled & (device_col_ids == column)
            return jnp.where(replace[:, None, None], left_block, updated)
        state = lax.map(update_device, (state, row_place, col_place, col_ids, coupled))
    state = jnp.where((row_ids >= 0)[:, :, None, None], state, 0.0)
    return state.reshape(values.shape)
```

```python
import jax
import jax.numpy as jnp
from jax import lax
from jax.experimental import pallas as pl
from jax.experimental.pallas import tpu as pltpu
from jax.sharding import PartitionSpec as P

B = 128
NB = 32
SLOTS = 68
HIGH = lax.Precision.HIGHEST
MESH = pl.DeviceIdType.MESH
F32 = jnp.float32
BF16 = jnp.bfloat16


def exchange_kernel(
    ids, coupled, values, left, right, lead, vbuf, vsem,
    zs, zr, xs, xr, os_, ys, yr, ss, sr, lxs, lxr, lys, lyr, lss, lsr,
):
    r = lax.axis_index("row")
    z = lax.axis_index("col")
    h = lax.rem(r, 2)
    x = lax.rem(r // 2, 4)
    y = r // 8
    row_of = lambda yy, xx, hh: yy * 8 + xx * 2 + hh
    up = lax.rem(z + 1, 8)
    down = lax.rem(z + 7, 8)
    sib = row_of(y, x, 1 - h)
    step = 1 - 2 * h
    xn = row_of(y, lax.rem(x + 4 + step, 4), h)
    xp = row_of(y, lax.rem(x + 4 - step, 4), h)
    yup = row_of(lax.rem(y + 1, 4), x, h)
    ydn = row_of(lax.rem(y + 3, 4), x, h)
    x0 = z // 2
    h0 = lax.rem(z, 2)
    dx = lax.rem(step * (x - x0) + 4, 4)
    is_source = (x == x0) & (h == h0)

    load = pltpu.make_async_copy(values, vbuf, vsem)

    @pl.when(z < 4)
    def _():
        load.start()

    barrier = pltpu.get_barrier_semaphore()
    for row, col in ((r, up), (r, down), (sib, z), (xn, z), (xp, z), (yup, z), (ydn, z)):
        pl.semaphore_signal(barrier, inc=1, device_id={"row": row, "col": col}, device_id_type=MESH)

    def scan(s, found):
        i = ids[s, 0]
        hit = ids[s, 1] == z
        return tuple(jnp.where(hit & (i == coupled[r, a]), s, found[a]) for a in range(4))

    found = lax.fori_loop(0, SLOTS, scan, (jnp.int32(-1),) * 4)
    pl.semaphore_wait(barrier, 7)

    @pl.when(z < 4)
    def _():
        load.wait()
        for a in range(4):
            block = vbuf[jnp.maximum(found[a], 0)]
            left[z, a] = jnp.where(found[a] >= 0, block, 0.0)

    def copy(src, dst, ssem, rsem, row, col):
        return pltpu.make_async_remote_copy(
            src_ref=src, dst_ref=dst, send_sem=ssem, recv_sem=rsem,
            device_id={"row": row, "col": col}, device_id_type=MESH,
        )

    sends = []

    def send(cond, desc):
        if cond is None:
            desc.start()
            sends.append((None, desc))
        else:
            pl.when(cond)(desc.start)
            sends.append((cond, desc))

    def recv(cond, desc):
        if cond is None:
            desc.wait_recv()
        else:
            pl.when(cond)(desc.wait_recv)

    ku = [lax.rem(jnp.minimum(z, 3) - m + 4, 4) for m in range(4)]
    kd = [lax.rem(jnp.where(z < 4, z, 0) + m, 4) for m in range(4)]
    km = [jnp.where(h == 0, ku[m], kd[m]) for m in range(4)]

    def z_event(m, q):
        for half, k, to in ((0, ku[m], up), (1, kd[m], down)):
            a = 2 * half + q
            block = left.at[k, a]
            desc = copy(block, block, zs.at[k, a], zr.at[k, a], r, to)
            recv(k != z, desc)
            send(to != k, desc)
            target = right.at[y, k, a]
            send(
                is_source & (h != half),
                copy(block, target, os_.at[k, q], xr.at[k, q], sib, z),
            )

    def forward(yy, m, q):
        a = 2 * h + q
        block = right.at[yy, km[m], a]
        send(None, copy(block, block, ss.at[yy, km[m], q], sr.at[yy, km[m], q], sib, z))

    def x_event(m, q):
        k = km[m]
        a = 2 * h + q
        block = right.at[y, k, a]
        desc = copy(block, block, xs.at[k, q], xr.at[k, q], xn, z)

        @pl.when(is_source)
        def _():
            right[y, k, a] = left[k, a]

        recv(jnp.logical_not(is_source), desc)
        send(dx < 3, desc)
        send(None, copy(block, block, ys.at[y, k, q], yr.at[y, k, q], ydn if q else yup, z))
        forward(y, m, q)

    def y_event(s, m, q):
        yy = lax.rem(y + s, 4) if q else lax.rem(y + 4 - s, 4)
        k = km[m]
        block = right.at[yy, k, 2 * h + q]
        desc = copy(block, block, ys.at[yy, k, q], yr.at[yy, k, q], ydn if q else yup, z)
        recv(None, desc)
        if s < 3:
            send(None, desc)
        forward(yy, m, q)

    def lead_x(i):
        hi, xi = i % 2, i // 2
        di = lax.rem(step * (x - xi) + 4, 4)
        mine = (h == hi) & (y == 0)
        block = lead.at[i, 0 : i + 1]

        @pl.when(mine & (di == 0))
        def _():
            for k in range(i + 1):
                lead[i, k] = left[k, 0]

        desc = copy(block, block, lxs.at[i], lxr.at[i], xn, z)
        recv(mine & (di > 0), desc)
        send(mine & (di < 3), desc)
        send(mine, copy(block, block, lys.at[i, 0], lyr.at[i], yup, z))
        send(mine, copy(block, block, lys.at[i, 1], lyr.at[i], ydn, z))
        send(mine, copy(block, block, lss.at[i], lsr.at[i], sib, z))

    def lead_y(i):
        hi = i % 2
        mine = (h == hi) & (y > 0)
        block = lead.at[i, 0 : i + 1]
        desc = copy(block, block, lys.at[i, 0], lyr.at[i], yup, z)
        recv(mine, desc)
        send(mine & (y == 1), desc)
        send(mine, copy(block, block, lss.at[i], lsr.at[i], sib, z))

    def lead_s(i):
        block = lead.at[i, 0 : i + 1]
        recv(h != i % 2, copy(block, block, lss.at[i], lsr.at[i], sib, z))

    events = []
    for m in range(4):
        for q in range(2):
            t = 2 * m + q
            events.append((t, 0, lambda m=m, q=q: z_event(m, q)))
            events.append((t + 2.5, 1, lambda m=m, q=q: x_event(m, q)))
            for s in range(1, 4):
                events.append((t + 2.5 + 2 * s, 2, lambda s=s, m=m, q=q: y_event(s, m, q)))
    for i in range(4):
        events.append((7 + 0.1 * i, 3, lambda i=i: lead_x(i)))
        events.append((10 + 0.1 * i, 4, lambda i=i: lead_y(i)))
        events.append((20 + 0.1 * i, 5, lambda i=i: lead_s(i)))
    for _, _, run in sorted(events, key=lambda e: e[:2]):
        run()

    for yy in range(4):
        for k in range(4):
            for q in range(2):
                block = right.at[yy, k, 2 * (1 - h) + q]
                copy(block, block, ss.at[yy, k, q], sr.at[yy, k, q], sib, z).wait_recv()
    for cond, desc in sends:
        if cond is None:
            desc.wait_send()
        else:
            pl.when(cond)(desc.wait_send)


def exchange(ids, coupled, values):
    dma = pltpu.SemaphoreType.DMA
    vmem = pl.BlockSpec(memory_space=pltpu.VMEM)
    return pl.pallas_call(
        exchange_kernel,
        out_shape=(
            jax.ShapeDtypeStruct((4, 4, B, B), F32),
            jax.ShapeDtypeStruct((4, 4, 4, B, B), F32),
            jax.ShapeDtypeStruct((4, 4, B, B), F32),
        ),
        in_specs=[
            pl.BlockSpec(memory_space=pltpu.SMEM),
            pl.BlockSpec(memory_space=pltpu.SMEM),
            pl.BlockSpec(memory_space=pl.ANY),
        ],
        out_specs=(vmem, vmem, vmem),
        scratch_shapes=[
            pltpu.VMEM((SLOTS, B, B), F32),
            dma,
            dma((4, 4)), dma((4, 4)),
            dma((4, 2)), dma((4, 2)), dma((4, 2)),
            dma((4, 4, 2)), dma((4, 4, 2)),
            dma((4, 4, 2)), dma((4, 4, 2)),
            dma((4,)), dma((4,)),
            dma((4, 2)), dma((4,)),
            dma((4,)), dma((4,)),
        ],
        compiler_params=pltpu.CompilerParams(
            collective_id=0, has_side_effects=True, vmem_limit_bytes=40 << 20
        ),
        name="exchange",
    )(ids, coupled, values)


def eliminate(m2):
    sub = lax.broadcasted_iota(jnp.int32, (8, B), 0)
    nt = NB // 8
    for p in range(B // NB):
        b = NB * p
        T = [[m2[b + 8 * i : b + 8 * i + 8, B * t : B * t + B] for t in range(2)] for i in range(nt)]
        for u in range(nt):
            cb = b + 8 * u
            C = {
                (i, j): jnp.broadcast_to(T[i][0][:, cb + j : cb + j + 1], (8, B))
                for i in range(u, nt)
                for j in range(8)
            }
            sc = jnp.ones((8, B), F32)
            for j in range(8):
                piv = jnp.broadcast_to(C[u, j][j : j + 1, :], (8, B))
                inv = 1.0 / piv
                sc = jnp.where(sub == j, lax.rsqrt(piv), sc)
                rows = [jnp.broadcast_to(T[u][t][j : j + 1, :], (8, B)) for t in range(2)]
                cs = {jj: jnp.broadcast_to(C[u, jj][j : j + 1, :], (8, B)) for jj in range(j + 1, 8)}
                for i in range(u, nt):
                    m = C[i, j] * inv
                    if i == u:
                        if j == 7:
                            continue
                        m = jnp.where(sub > j, m, 0.0)
                    for jj in range(j + 1, 8):
                        C[i, jj] = C[i, jj] - m * cs[jj]
                    for t in range(2):
                        T[i][t] = T[i][t] - m * rows[t]
            for t in range(2):
                T[u][t] = T[u][t] * sc
        for i in range(nt):
            for t in range(2):
                m2[b + 8 * i : b + 8 * i + 8, B * t : B * t + B] = T[i][t]
        if b + NB < B:
            R = m2[b : b + NB, :]
            g = lax.dot_general(
                R[:, b + NB : B], R, (((0,), (0,)), ((), ())), precision=HIGH, preferred_element_type=F32
            )
            m2[b + NB : B, :] = m2[b + NB : B, :] - g


def factor_lead(lead, m2, s, e, diag):
    n = 4
    ri = lax.broadcasted_iota(jnp.int32, (B, B), 0)
    ci = lax.broadcasted_iota(jnp.int32, (B, B), 1)
    eye = jnp.where(ri == ci, 1.0, 0.0).astype(F32)
    for i in range(n):
        s[B * i : B * i + B, B * i : B * i + B] = lead[i, i]
        for k in range(i):
            s[B * k : B * k + B, B * i : B * i + B] = lead[i, k].T
    e[...] = jnp.zeros_like(e)
    for k in range(n):
        a, z = B * k, B * k + B
        m2[:, :B] = s[a:z, a:z]
        m2[:, B:] = eye
        eliminate(m2)
        li = jnp.where(ri >= ci, m2[:, B:], 0.0)
        diag[k] = jnp.where(ri >= ci, m2[:, :B].T, 0.0)
        parts = []
        if k < n - 1:
            parts.append(s[a:z, z:])
        if k > 0:
            parts.append(e[a:z, :a])
        R = jnp.dot(li, jnp.concatenate(parts, axis=1), precision=HIGH, preferred_element_type=F32)
        w = (n - 1 - k) * B
        if k > 0:
            e[a:z, :a] = R[:, w:]
        e[a:z, a:z] = li
        if k < n - 1:
            full = jnp.concatenate([R, li], axis=1)
            g = lax.dot_general(
                R[:, :w], full, (((0,), (0,)), ((), ())), precision=HIGH, preferred_element_type=F32
            )
            s[z:, z:] = s[z:, z:] - g[:, :w]
            e[z:, :z] = e[z:, :z] - g[:, w:]


def split(v):
    hi = v.astype(BF16)
    return hi, (v - hi.astype(F32)).astype(BF16)


def dot_nt(a, b):
    (ah, al), (bh, bl) = a, b
    mm = lambda p, q: lax.dot_general(p, q, (((1,), (1,)), ((), ())), preferred_element_type=F32)
    return mm(ah, bh) + (mm(ah, bl) + mm(al, bh))


def finish_kernel(
    ids, coupled, values, left, right, lead, out,
    vbuf, lbuf, rbuf, obuf, m2, s, e, diag, ehi, elo, whi, wlo, g, vsem, lsem, rsem, osem,
):
    r = lax.axis_index("row")
    loads = [
        pltpu.make_async_copy(left, lbuf, lsem),
        pltpu.make_async_copy(right, rbuf, rsem),
        pltpu.make_async_copy(values, vbuf, vsem),
    ]
    for load in loads:
        load.start()
    factor_lead(lead, m2, s, e, diag)
    hi, lo = split(e[...])
    ehi[...] = hi
    elo[...] = lo

    def factor_rows(blocks):
        cat = [blocks[k].reshape(4 * B, B) for k in range(4)]
        parts = [split(c) for c in cat]
        xh = jnp.concatenate([p[0] for p in parts], axis=1)
        xl = jnp.concatenate([p[1] for p in parts], axis=1)
        h = 2 * B
        w0 = dot_nt((xh[:, :h], xl[:, :h]), (ehi[:h, :h], elo[:h, :h]))
        w1 = dot_nt((xh, xl), (ehi[h:, :], elo[h:, :]))
        return jnp.concatenate([w0, w1], axis=1)

    loads[0].wait()
    wl = factor_rows(lbuf)
    for n in range(4):
        for a in range(4):
            g[64 + 4 * n + a] = -wl[B * a : B * a + B, B * n : B * n + B]
    g[80] = jnp.zeros((B, B), F32)

    @pl.when(r < 4)
    def _():
        g[64 + 4 * r] = -diag[r]

    hi, lo = split(wl)
    whi[...] = hi
    wlo[...] = lo
    loads[1].wait()

    @pl.loop(0, 4)
    def _(y):
        wr = factor_rows(rbuf.at[y])
        p = dot_nt((whi[...], wlo[...]), split(wr))
        for b in range(4):
            for a in range(4):
                g[(y * 4 + b) * 4 + a] = p[B * a : B * a + B, B * b : B * b + B]

    loads[2].wait()

    @pl.loop(0, SLOTS)
    def _(slot):
        i = ids[slot, 0]
        j = ids[slot, 1]
        a = jnp.int32(0)
        own = jnp.int32(0)
        b = jnp.int32(0)
        r2 = j & 31
        for n in range(4):
            hit = i == coupled[r, n]
            a = jnp.where(hit, n, a)
            own = jnp.where(hit, 1, own)
            b = jnp.where(j == coupled[r2, n], n, b)
        found = own == 1
        trailing = found & (j >= 4)
        panel = found & (j < 4)
        place = jnp.where(trailing, ((r2 // 8) * 4 + b) * 4 + a, jnp.where(panel, 64 + 4 * j + a, 80))
        keep = (i >= 0) & jnp.logical_not(panel)
        obuf[slot] = jnp.where(keep, vbuf[slot], 0.0) - g[place]
        pltpu.make_async_copy(obuf.at[slot], out.at[slot], osem).start()

    pltpu.make_async_copy(obuf, out, osem).wait()


def finish(ids, coupled, values, left, right, lead):
    smem = pl.BlockSpec(memory_space=pltpu.SMEM)
    anywhere = pl.BlockSpec(memory_space=pl.ANY)
    dma = pltpu.SemaphoreType.DMA
    return pl.pallas_call(
        finish_kernel,
        out_shape=jax.ShapeDtypeStruct((SLOTS, B, B), F32),
        in_specs=[smem, smem, anywhere, anywhere, anywhere, pl.BlockSpec(memory_space=pltpu.VMEM)],
        out_specs=anywhere,
        scratch_shapes=[
            pltpu.VMEM((SLOTS, B, B), F32),
            pltpu.VMEM((4, 4, B, B), F32),
            pltpu.VMEM((4, 4, 4, B, B), F32),
            pltpu.VMEM((SLOTS, B, B), F32),
            pltpu.VMEM((B, 2 * B), F32),
            pltpu.VMEM((512, 512), F32),
            pltpu.VMEM((512, 512), F32),
            pltpu.VMEM((4, B, B), F32),
            pltpu.VMEM((512, 512), BF16),
            pltpu.VMEM((512, 512), BF16),
            pltpu.VMEM((512, 512), BF16),
            pltpu.VMEM((512, 512), BF16),
            pltpu.VMEM((81, B, B), F32),
            dma, dma, dma, dma,
        ],
        compiler_params=pltpu.CompilerParams(vmem_limit_bytes=48 << 20),
        name="finish",
    )(ids, coupled, values, left, right, lead)


def body(values, block_ids, coupled_rows):
    ids = block_ids[0, 0]
    left, right, lead = exchange(ids, coupled_rows, values[0, 0])
    out = finish(ids, coupled_rows, values[0, 0], left, right, lead)
    return out[None, None]


def solution(mesh):
    placed = (P("row", "col", None, None, None), P("row", "col", None, None), P())
    return jax.shard_map(
        body,
        mesh=mesh,
        in_specs=placed,
        out_specs=P("row", "col", None, None, None),
        check_vma=False,
    )
```

```python
import jax
import jax.numpy as jnp
from jax import lax
from jax.experimental import pallas as pl
from jax.experimental.pallas import tpu as pltpu
from jax.sharding import PartitionSpec as P

B = 128
NB = 32
SLOTS = 68
HIGH = lax.Precision.HIGHEST
MESH = pl.DeviceIdType.MESH
F32 = jnp.float32
BF16 = jnp.bfloat16


def exchange_kernel(
    ids, coupled, values, left, right, lead, vbuf, vsem,
    zus, zds, zr, xs, xr, os_, ys, yr, ss, sr, l1s, l1r, l2s, l2r, l3s, l3r, lss, lsr,
):
    r = lax.axis_index("row")
    z = lax.axis_index("col")
    h = lax.rem(r, 2)
    x = lax.rem(r // 2, 4)
    y = r // 8
    up = lax.rem(z + 1, 8)
    down = lax.rem(z + 7, 8)
    sib = r + 1 - 2 * h
    xo = [y * 8 + lax.rem(x + d, 4) * 2 + h for d in (1, 3, 2)]
    yo = [lax.rem(y + d, 4) * 8 + x * 2 + h for d in (1, 3, 2)]
    origin = x == z // 2
    source = origin & (h == lax.rem(z, 2))
    lead_row = r < 4
    true = r >= 0

    load = pltpu.make_async_copy(values, vbuf, vsem)
    pl.when(z < 4)(load.start)

    barrier = pltpu.get_barrier_semaphore()

    def greet(row, col):
        pl.semaphore_signal(barrier, inc=1, device_id={"row": row, "col": col}, device_id_type=MESH)

    greet(r, up)
    greet(r, down)
    greet(sib, z)
    for t in xo + yo:
        greet(t, z)

    @pl.when(lead_row)
    def _():
        for d in range(2, 7):
            greet(r, lax.rem(z + d, 8))

    def scan(s, found):
        i = ids[s, 0]
        hit = ids[s, 1] == z
        return tuple(jnp.where(hit & (i == coupled[r, a]), s, found[a]) for a in range(4))

    found = lax.fori_loop(0, SLOTS, scan, (jnp.int32(-1),) * 4)
    pl.semaphore_wait(barrier, jnp.where(lead_row, 14, 9))

    @pl.when(z < 4)
    def _():
        load.wait()
        for a in range(4):
            block = vbuf[jnp.maximum(found[a], 0)]
            left[z, a] = jnp.where(found[a] >= 0, block, 0.0)

    def copy(src, dst, ssem, rsem, row, col):
        return pltpu.make_async_remote_copy(
            src_ref=src, dst_ref=dst, send_sem=ssem, recv_sem=rsem,
            device_id={"row": row, "col": col}, device_id_type=MESH,
        )

    sends = []

    def send(cond, desc):
        pl.when(cond)(desc.start)
        sends.append((cond, desc))

    half = pl.ds(2 * h, 2)
    other = pl.ds(2 - 2 * h, 2)

    def travellers(d):
        if d == 0:
            return [(jnp.minimum(z, 3), z < 4, true, true)]
        ku = z - d
        vu = (ku >= 0) & (ku <= 3) & ((ku >= 2) | (z <= 3))
        kd = lax.rem(z + d, 8)
        vd = (kd <= 3) & jnp.where(kd >= 2, z < kd, (z < kd) | (z >= 4))
        return [
            (jnp.clip(ku, 0, 3), vu, jnp.where(ku >= 2, z < 7, z < 3), None),
            (jnp.minimum(kd, 3), vd, None, jnp.where(kd >= 2, z > 0, z != 4)),
        ]

    def spread(k, cond):
        block = right.at[y, k, half]
        for n in range(3):
            send(cond, copy(block, block, ys.at[k, n], yr.at[y, k], yo[n], z))
        send(cond, copy(block, block, ss.at[y, k], sr.at[y, k], sib, z))

    def spread_x(k, cond):
        block = right.at[y, k, half]
        for n in range(3):
            send(cond & origin, copy(block, block, xs.at[k, n], xr.at[k], xo[n], z))

    def z_event(d):
        for k, valid, go_up, go_down in travellers(d):
            for a in range(4):
                block = left.at[k, a]
                if d > 0:
                    pl.when(valid)(copy(block, block, zus.at[k, a], zr.at[k, a], r, up).wait_recv)
                if go_up is not None:
                    send(valid & go_up, copy(block, block, zus.at[k, a], zr.at[k, a], r, up))
                if go_down is not None:
                    send(valid & go_down, copy(block, block, zds.at[k, a], zr.at[k, a], r, down))
            mine = valid & source

            @pl.when(mine)
            def _():
                right[y, k, half] = left[k, half]

            send(mine, copy(left.at[k, other], right.at[y, k, other], os_.at[k], xr.at[k], sib, z))
            spread_x(k, mine)
            spread(k, mine)

    def x_event(d):
        for k, valid, _, _ in travellers(d):
            block = right.at[y, k, half]
            mine = valid & jnp.logical_not(source)
            pl.when(mine)(copy(block, block, os_.at[k], xr.at[k], sib, z).wait_recv)
            spread_x(k, mine)
            spread(k, mine)

    def y_event(d, n):
        yy = lax.rem(y + (1, 3, 2)[n], 4)
        for k, valid, _, _ in travellers(d):
            block = right.at[yy, k, half]
            pl.when(valid)(copy(block, block, ys.at[k, n], yr.at[yy, k], yo[n], z).wait_recv)
            send(valid, copy(block, block, ss.at[yy, k], sr.at[yy, k], sib, z))

    def lead_z():
        mine = lead_row & (z <= r)
        i = jnp.minimum(r, 3)
        k = jnp.minimum(z, 3)
        block = lead.at[i, k]

        @pl.when(mine)
        def _():
            lead[i, k] = left[k, 0]

        for d in range(1, 8):
            send(mine, copy(block, block, l1s.at[d - 1], l1r.at[k], r, lax.rem(z + d, 8)))

    def lead_x(i):
        mine = r == i
        for k in range(i + 1):
            block = lead.at[i, k]
            pl.when(mine & (z != k))(copy(block, block, l1s.at[0], l1r.at[k], r, up).wait_recv)
        row = lead.at[i, 0 : i + 1]
        for n in range(3):
            send(mine, copy(row, row, l2s.at[i, n], l2r.at[i], xo[n], z))
        for n in range(3):
            send(mine, copy(row, row, l3s.at[i, n], l3r.at[i], yo[n], z))
        send(mine, copy(row, row, lss.at[i], lsr.at[i], sib, z))

    def lead_y(i):
        row = lead.at[i, 0 : i + 1]
        mine = (y == 0) & (h == i % 2) & (x != i // 2)
        pl.when(mine)(copy(row, row, l2s.at[i, 0], l2r.at[i], xo[0], z).wait_recv)
        for n in range(3):
            send(mine, copy(row, row, l3s.at[i, n], l3r.at[i], yo[n], z))
        send(mine, copy(row, row, lss.at[i], lsr.at[i], sib, z))

    def lead_s(i):
        row = lead.at[i, 0 : i + 1]
        mine = (y > 0) & (h == i % 2)
        pl.when(mine)(copy(row, row, l3s.at[i, 0], l3r.at[i], yo[0], z).wait_recv)
        send(mine, copy(row, row, lss.at[i], lsr.at[i], sib, z))

    lead_z()
    for t in range(8):
        if t <= 5:
            z_event(t)
        if t == 1:
            for i in range(4):
                lead_x(i)
        if t == 2:
            for i in range(4):
                lead_y(i)
        if t == 3:
            for i in range(4):
                lead_s(i)
        if 1 <= t <= 6:
            x_event(t - 1)
        if t >= 2:
            for n in range(3):
                y_event(t - 2, n)

    for i in range(4):
        row = lead.at[i, 0 : i + 1]
        pl.when(h != i % 2)(copy(row, row, lss.at[i], lsr.at[i], sib, z).wait_recv)
    for yy in range(4):
        for k in range(4):
            block = right.at[yy, k, other]
            copy(block, block, ss.at[yy, k], sr.at[yy, k], sib, z).wait_recv()
    for cond, desc in sends:
        pl.when(cond)(desc.wait_send)


def exchange(ids, coupled, values):
    dma = pltpu.SemaphoreType.DMA
    vmem = pl.BlockSpec(memory_space=pltpu.VMEM)
    return pl.pallas_call(
        exchange_kernel,
        out_shape=(
            jax.ShapeDtypeStruct((4, 4, B, B), F32),
            jax.ShapeDtypeStruct((4, 4, 4, B, B), F32),
            jax.ShapeDtypeStruct((4, 4, B, B), F32),
        ),
        in_specs=[
            pl.BlockSpec(memory_space=pltpu.SMEM),
            pl.BlockSpec(memory_space=pltpu.SMEM),
            pl.BlockSpec(memory_space=pl.ANY),
        ],
        out_specs=(vmem, vmem, vmem),
        scratch_shapes=[
            pltpu.VMEM((SLOTS, B, B), F32),
            dma,
            dma((4, 4)), dma((4, 4)), dma((4, 4)),
            dma((4, 3)), dma((4,)), dma((4,)),
            dma((4, 3)), dma((4, 4)),
            dma((4, 4)), dma((4, 4)),
            dma((7,)), dma((4,)),
            dma((4, 3)), dma((4,)),
            dma((4, 3)), dma((4,)),
            dma((4,)), dma((4,)),
        ],
        compiler_params=pltpu.CompilerParams(
            collective_id=0, has_side_effects=True, vmem_limit_bytes=40 << 20
        ),
        name="exchange",
    )(ids, coupled, values)


def eliminate(m2):
    sub = lax.broadcasted_iota(jnp.int32, (8, B), 0)
    nt = NB // 8
    for p in range(B // NB):
        b = NB * p
        T = [[m2[b + 8 * i : b + 8 * i + 8, B * t : B * t + B] for t in range(2)] for i in range(nt)]
        for u in range(nt):
            cb = b + 8 * u
            C = {
                (i, j): jnp.broadcast_to(T[i][0][:, cb + j : cb + j + 1], (8, B))
                for i in range(u, nt)
                for j in range(8)
            }
            sc = jnp.ones((8, B), F32)
            for j in range(8):
                piv = jnp.broadcast_to(C[u, j][j : j + 1, :], (8, B))
                inv = 1.0 / piv
                sc = jnp.where(sub == j, lax.rsqrt(piv), sc)
                rows = [jnp.broadcast_to(T[u][t][j : j + 1, :], (8, B)) for t in range(2)]
                cs = {jj: jnp.broadcast_to(C[u, jj][j : j + 1, :], (8, B)) for jj in range(j + 1, 8)}
                for i in range(u, nt):
                    m = C[i, j] * inv
                    if i == u:
                        if j == 7:
                            continue
                        m = jnp.where(sub > j, m, 0.0)
                    for jj in range(j + 1, 8):
                        C[i, jj] = C[i, jj] - m * cs[jj]
                    for t in range(2):
                        T[i][t] = T[i][t] - m * rows[t]
            for t in range(2):
                T[u][t] = T[u][t] * sc
        for i in range(nt):
            for t in range(2):
                m2[b + 8 * i : b + 8 * i + 8, B * t : B * t + B] = T[i][t]
        if b + NB < B:
            R = m2[b : b + NB, :]
            g = lax.dot_general(
                R[:, b + NB : B], R, (((0,), (0,)), ((), ())), precision=HIGH, preferred_element_type=F32
            )
            m2[b + NB : B, :] = m2[b + NB : B, :] - g


def factor_lead(lead, m2, s, e, diag):
    n = 4
    ri = lax.broadcasted_iota(jnp.int32, (B, B), 0)
    ci = lax.broadcasted_iota(jnp.int32, (B, B), 1)
    eye = jnp.where(ri == ci, 1.0, 0.0).astype(F32)
    for i in range(n):
        s[B * i : B * i + B, B * i : B * i + B] = lead[i, i]
        for k in range(i):
            s[B * k : B * k + B, B * i : B * i + B] = lead[i, k].T
    e[...] = jnp.zeros_like(e)
    for k in range(n):
        a, z = B * k, B * k + B
        m2[:, :B] = s[a:z, a:z]
        m2[:, B:] = eye
        eliminate(m2)
        li = jnp.where(ri >= ci, m2[:, B:], 0.0)
        diag[k] = jnp.where(ri >= ci, m2[:, :B].T, 0.0)
        parts = []
        if k < n - 1:
            parts.append(s[a:z, z:])
        if k > 0:
            parts.append(e[a:z, :a])
        R = jnp.dot(li, jnp.concatenate(parts, axis=1), precision=HIGH, preferred_element_type=F32)
        w = (n - 1 - k) * B
        if k > 0:
            e[a:z, :a] = R[:, w:]
        e[a:z, a:z] = li
        if k < n - 1:
            full = jnp.concatenate([R, li], axis=1)
            g = lax.dot_general(
                R[:, :w], full, (((0,), (0,)), ((), ())), precision=HIGH, preferred_element_type=F32
            )
            s[z:, z:] = s[z:, z:] - g[:, :w]
            e[z:, :z] = e[z:, :z] - g[:, w:]


def split(v):
    hi = v.astype(BF16)
    return hi, (v - hi.astype(F32)).astype(BF16)


def dot_nt(a, b):
    (ah, al), (bh, bl) = a, b
    mm = lambda p, q: lax.dot_general(p, q, (((1,), (1,)), ((), ())), preferred_element_type=F32)
    return mm(ah, bh) + (mm(ah, bl) + mm(al, bh))


def finish_kernel(
    ids, coupled, values, left, right, lead, out,
    vbuf, lbuf, rbuf, obuf, m2, s, e, diag, ehi, elo, whi, wlo, g, vsem, lsem, rsem, osem,
):
    r = lax.axis_index("row")
    loads = [
        pltpu.make_async_copy(left, lbuf, lsem),
        pltpu.make_async_copy(right, rbuf, rsem),
        pltpu.make_async_copy(values, vbuf, vsem),
    ]
    for load in loads:
        load.start()
    factor_lead(lead, m2, s, e, diag)
    hi, lo = split(e[...])
    ehi[...] = hi
    elo[...] = lo

    def factor_rows(blocks):
        cat = [blocks[k].reshape(4 * B, B) for k in range(4)]
        parts = [split(c) for c in cat]
        xh = jnp.concatenate([p[0] for p in parts], axis=1)
        xl = jnp.concatenate([p[1] for p in parts], axis=1)
        h = 2 * B
        w0 = dot_nt((xh[:, :h], xl[:, :h]), (ehi[:h, :h], elo[:h, :h]))
        w1 = dot_nt((xh, xl), (ehi[h:, :], elo[h:, :]))
        return jnp.concatenate([w0, w1], axis=1)

    loads[0].wait()
    wl = factor_rows(lbuf)
    for n in range(4):
        for a in range(4):
            g[64 + 4 * n + a] = -wl[B * a : B * a + B, B * n : B * n + B]
    g[80] = jnp.zeros((B, B), F32)

    @pl.when(r < 4)
    def _():
        g[64 + 4 * r] = -diag[r]

    hi, lo = split(wl)
    whi[...] = hi
    wlo[...] = lo
    loads[1].wait()

    @pl.loop(0, 4)
    def _(y):
        wr = factor_rows(rbuf.at[y])
        p = dot_nt((whi[...], wlo[...]), split(wr))
        for b in range(4):
            for a in range(4):
                g[(y * 4 + b) * 4 + a] = p[B * a : B * a + B, B * b : B * b + B]

    loads[2].wait()

    @pl.loop(0, SLOTS)
    def _(slot):
        i = ids[slot, 0]
        j = ids[slot, 1]
        a = jnp.int32(0)
        own = jnp.int32(0)
        b = jnp.int32(0)
        r2 = j & 31
        for n in range(4):
            hit = i == coupled[r, n]
            a = jnp.where(hit, n, a)
            own = jnp.where(hit, 1, own)
            b = jnp.where(j == coupled[r2, n], n, b)
        found = own == 1
        trailing = found & (j >= 4)
        panel = found & (j < 4)
        place = jnp.where(trailing, ((r2 // 8) * 4 + b) * 4 + a, jnp.where(panel, 64 + 4 * j + a, 80))
        keep = (i >= 0) & jnp.logical_not(panel)
        obuf[slot] = jnp.where(keep, vbuf[slot], 0.0) - g[place]
        pltpu.make_async_copy(obuf.at[slot], out.at[slot], osem).start()

    pltpu.make_async_copy(obuf, out, osem).wait()


def finish(ids, coupled, values, left, right, lead):
    smem = pl.BlockSpec(memory_space=pltpu.SMEM)
    anywhere = pl.BlockSpec(memory_space=pl.ANY)
    dma = pltpu.SemaphoreType.DMA
    return pl.pallas_call(
        finish_kernel,
        out_shape=jax.ShapeDtypeStruct((SLOTS, B, B), F32),
        in_specs=[smem, smem, anywhere, anywhere, anywhere, pl.BlockSpec(memory_space=pltpu.VMEM)],
        out_specs=anywhere,
        scratch_shapes=[
            pltpu.VMEM((SLOTS, B, B), F32),
            pltpu.VMEM((4, 4, B, B), F32),
            pltpu.VMEM((4, 4, 4, B, B), F32),
            pltpu.VMEM((SLOTS, B, B), F32),
            pltpu.VMEM((B, 2 * B), F32),
            pltpu.VMEM((512, 512), F32),
            pltpu.VMEM((512, 512), F32),
            pltpu.VMEM((4, B, B), F32),
            pltpu.VMEM((512, 512), BF16),
            pltpu.VMEM((512, 512), BF16),
            pltpu.VMEM((512, 512), BF16),
            pltpu.VMEM((512, 512), BF16),
            pltpu.VMEM((81, B, B), F32),
            dma, dma, dma, dma,
        ],
        compiler_params=pltpu.CompilerParams(vmem_limit_bytes=48 << 20),
        name="finish",
    )(ids, coupled, values, left, right, lead)


def body(values, block_ids, coupled_rows):
    ids = block_ids[0, 0]
    left, right, lead = exchange(ids, coupled_rows, values[0, 0])
    out = finish(ids, coupled_rows, values[0, 0], left, right, lead)
    return out[None, None]


def solution(mesh):
    placed = (P("row", "col", None, None, None), P("row", "col", None, None), P())
    return jax.shard_map(
        body,
        mesh=mesh,
        in_specs=placed,
        out_specs=P("row", "col", None, None, None),
        check_vma=False,
    )
```

```python
import jax
import jax.numpy as jnp
from jax import lax
from jax.experimental import pallas as pl
from jax.experimental.pallas import tpu as pltpu
from jax.sharding import PartitionSpec as P

B = 128
NB = 32
SLOTS = 68
HIGH = lax.Precision.HIGHEST
MESH = pl.DeviceIdType.MESH
F32 = jnp.float32
BF16 = jnp.bfloat16


def exchange_kernel(
    ids, coupled, values, left, right, inverse, diag, vbuf, lead, m2, s, vsem,
    zus, zds, zr, xs, xr, os_, ys, yr, yfs, yfr, ss, sr, l1s, l1r, l2s, l2r, l3s, l3r, lss, lsr,
):
    r = lax.axis_index("row")
    z = lax.axis_index("col")
    h = lax.rem(r, 2)
    x = lax.rem(r // 2, 4)
    y = r // 8
    up = lax.rem(z + 1, 8)
    down = lax.rem(z + 7, 8)
    sib = r + 1 - 2 * h
    xo = [y * 8 + lax.rem(x + d, 4) * 2 + h for d in (1, 3, 2)]
    yo = [lax.rem(y + d, 4) * 8 + x * 2 + h for d in (1, 3, 2)]
    origin = x == z // 2
    source = origin & (h == lax.rem(z, 2))
    lead_row = r < 4
    true = r >= 0

    load = pltpu.make_async_copy(values, vbuf, vsem)
    pl.when(z < 4)(load.start)

    barrier = pltpu.get_barrier_semaphore()

    def greet(row, col):
        pl.semaphore_signal(barrier, inc=1, device_id={"row": row, "col": col}, device_id_type=MESH)

    greet(r, up)
    greet(r, down)
    greet(sib, z)
    for t in xo + yo:
        greet(t, z)

    @pl.when(lead_row)
    def _():
        for d in range(2, 7):
            greet(r, lax.rem(z + d, 8))

    def scan(slot, found):
        i = ids[0, slot]
        hit = ids[1, slot] == z
        return tuple(jnp.where(hit & (i == coupled[a, r]), slot, found[a]) for a in range(4))

    found = lax.fori_loop(0, SLOTS, scan, (jnp.int32(-1),) * 4)
    pl.semaphore_wait(barrier, jnp.where(lead_row, 14, 9))

    @pl.when(z < 4)
    def _():
        load.wait()
        for a in range(4):
            block = vbuf[jnp.maximum(found[a], 0)]
            left[z, a] = jnp.where(found[a] >= 0, block, 0.0)

    def copy(src, dst, ssem, rsem, row, col):
        return pltpu.make_async_remote_copy(
            src_ref=src, dst_ref=dst, send_sem=ssem, recv_sem=rsem,
            device_id={"row": row, "col": col}, device_id_type=MESH,
        )

    sends = []

    def send(cond, desc):
        pl.when(cond)(desc.start)
        sends.append((cond, desc))

    half = pl.ds(2 * h, 2)
    other = pl.ds(2 - 2 * h, 2)

    def travellers(d):
        if d == 0:
            return [(jnp.minimum(z, 3), z < 4, true, true)]
        ku = z - d
        vu = (ku >= 0) & (ku <= 3) & ((ku >= 2) | (z <= 3))
        kd = lax.rem(z + d, 8)
        vd = (kd <= 3) & jnp.where(kd >= 2, z < kd, (z < kd) | (z >= 4))
        return [
            (jnp.clip(ku, 0, 3), vu, jnp.where(ku >= 2, z < 7, z < 3), None),
            (jnp.minimum(kd, 3), vd, None, jnp.where(kd >= 2, z > 0, z != 4)),
        ]

    def spread(k, cond):
        block = right.at[y, k, half]
        for n in range(2):
            send(cond, copy(block, block, ys.at[k, n], yr.at[y, k], yo[n], z))
        send(cond, copy(block, block, ss.at[y, k], sr.at[y, k], sib, z))

    def spread_x(k, cond):
        block = right.at[y, k, half]
        for n in range(3):
            send(cond & origin, copy(block, block, xs.at[k, n], xr.at[k], xo[n], z))

    def z_event(d):
        for k, valid, go_up, go_down in travellers(d):
            for a in range(4):
                block = left.at[k, a]
                if d > 0:
                    pl.when(valid)(copy(block, block, zus.at[k, a], zr.at[k, a], r, up).wait_recv)
                if go_up is not None:
                    send(valid & go_up, copy(block, block, zus.at[k, a], zr.at[k, a], r, up))
                if go_down is not None:
                    send(valid & go_down, copy(block, block, zds.at[k, a], zr.at[k, a], r, down))
            mine = valid & source

            @pl.when(mine)
            def _():
                right[y, k, half] = left[k, half]

            send(mine, copy(left.at[k, other], right.at[y, k, other], os_.at[k], xr.at[k], sib, z))
            spread_x(k, mine)
            spread(k, mine)

    def x_event(d):
        for k, valid, _, _ in travellers(d):
            block = right.at[y, k, half]
            mine = valid & jnp.logical_not(source)
            pl.when(mine)(copy(block, block, os_.at[k], xr.at[k], sib, z).wait_recv)
            spread_x(k, mine)
            spread(k, mine)

    def y_event(d, n):
        yy = lax.rem(y + (1, 3, 2)[n], 4)
        for k, valid, _, _ in travellers(d):
            block = right.at[yy, k, half]
            if n < 2:
                pl.when(valid)(copy(block, block, ys.at[k, n], yr.at[yy, k], yo[n], z).wait_recv)
                q = 1 - n
                part = right.at[yy, k, 2 * h + q]
                send(valid, copy(part, part, yfs.at[k, q], yfr.at[k, q], yo[1 - n], z))
            else:
                for q in range(2):
                    part = right.at[yy, k, 2 * h + q]
                    pl.when(valid)(copy(part, part, yfs.at[k, q], yfr.at[k, q], yo[q], z).wait_recv)
            send(valid, copy(block, block, ss.at[yy, k], sr.at[yy, k], sib, z))

    def lead_z():
        mine = lead_row & (z <= r)
        i = jnp.minimum(r, 3)
        k = jnp.minimum(z, 3)
        block = lead.at[i, k]

        @pl.when(mine)
        def _():
            lead[i, k] = left[k, 0]

        for d in range(1, 8):
            send(mine, copy(block, block, l1s.at[d - 1], l1r.at[k], r, lax.rem(z + d, 8)))

    def lead_x(i):
        mine = r == i
        for k in range(i + 1):
            block = lead.at[i, k]
            pl.when(mine & (z != k))(copy(block, block, l1s.at[0], l1r.at[k], r, up).wait_recv)
        row = lead.at[i, 0 : i + 1]
        for n in range(3):
            send(mine, copy(row, row, l2s.at[i, n], l2r.at[i], xo[n], z))
        for n in range(3):
            send(mine, copy(row, row, l3s.at[i, n], l3r.at[i], yo[n], z))
        send(mine, copy(row, row, lss.at[i], lsr.at[i], sib, z))

    def lead_y(i):
        row = lead.at[i, 0 : i + 1]
        mine = (y == 0) & (h == i % 2) & (x != i // 2)
        pl.when(mine)(copy(row, row, l2s.at[i, 0], l2r.at[i], xo[0], z).wait_recv)
        for n in range(3):
            send(mine, copy(row, row, l3s.at[i, n], l3r.at[i], yo[n], z))
        send(mine, copy(row, row, lss.at[i], lsr.at[i], sib, z))

    def lead_s(i):
        row = lead.at[i, 0 : i + 1]
        mine = (y > 0) & (h == i % 2)
        pl.when(mine)(copy(row, row, l3s.at[i, 0], l3r.at[i], yo[0], z).wait_recv)
        send(mine, copy(row, row, lss.at[i], lsr.at[i], sib, z))

    def lead_arrived(i):
        row = lead.at[i, 0 : i + 1]
        pl.when(h != i % 2)(copy(row, row, lss.at[i], lsr.at[i], sib, z).wait_recv)

    steps = factor_lead(lead, m2, s, inverse, diag, lead_arrived)

    def work(count):
        for _ in range(count):
            next(steps, None)

    lead_z()
    z_event(0)
    lead_x(0)
    z_event(1)
    for i in range(1, 4):
        lead_x(i)
    lead_y(0)
    x_event(0)
    z_event(2)
    for i in range(1, 4):
        lead_y(i)
    lead_s(0)
    x_event(1)
    for n in range(3):
        y_event(0, n)
    z_event(3)
    for i in range(1, 4):
        lead_s(i)
    work(4)
    x_event(2)
    for n in range(3):
        work(4)
        y_event(1, n)
    z_event(4)
    work(4)
    x_event(3)
    for n in range(3):
        work(4)
        y_event(2, n)
    z_event(5)
    work(4)
    x_event(4)
    for n in range(3):
        work(4)
        y_event(3, n)
    work(4)
    x_event(5)
    for n in range(3):
        work(4)
        y_event(4, n)
    for n in range(3):
        work(4)
        y_event(5, n)
    for _ in steps:
        pass

    for yy in range(4):
        for k in range(4):
            block = right.at[yy, k, other]
            copy(block, block, ss.at[yy, k], sr.at[yy, k], sib, z).wait_recv()
    for cond, desc in sends:
        pl.when(cond)(desc.wait_send)


def exchange(ids, coupled, values):
    dma = pltpu.SemaphoreType.DMA
    vmem = pl.BlockSpec(memory_space=pltpu.VMEM)
    return pl.pallas_call(
        exchange_kernel,
        out_shape=(
            jax.ShapeDtypeStruct((4, 4, B, B), F32),
            jax.ShapeDtypeStruct((4, 4, 4, B, B), F32),
            jax.ShapeDtypeStruct((512, 512), F32),
            jax.ShapeDtypeStruct((4, B, B), F32),
        ),
        in_specs=[
            pl.BlockSpec(memory_space=pltpu.SMEM),
            pl.BlockSpec(memory_space=pltpu.SMEM),
            pl.BlockSpec(memory_space=pltpu.HBM),
        ],
        out_specs=(vmem, vmem, vmem, vmem),
        scratch_shapes=[
            pltpu.VMEM((SLOTS, B, B), F32),
            pltpu.VMEM((4, 4, B, B), F32),
            pltpu.VMEM((B, 2 * B), F32),
            pltpu.VMEM((512, 512), F32),
            dma,
            dma((4, 4)), dma((4, 4)), dma((4, 4)),
            dma((4, 3)), dma((4,)), dma((4,)),
            dma((4, 2)), dma((4, 4)), dma((4, 2)), dma((4, 2)),
            dma((4, 4)), dma((4, 4)),
            dma((7,)), dma((4,)),
            dma((4, 3)), dma((4,)),
            dma((4, 3)), dma((4,)),
            dma((4,)), dma((4,)),
        ],
        compiler_params=pltpu.CompilerParams(
            collective_id=0, has_side_effects=True, vmem_limit_bytes=46 << 20
        ),
        name="exchange",
    )(ids, coupled, values)


def eliminate(m2):
    sub = lax.broadcasted_iota(jnp.int32, (8, B), 0)
    nt = NB // 8
    for p in range(B // NB):
        b = NB * p
        for u in range(nt):
            cb = b + 8 * u
            T = {
                (i, t): m2[b + 8 * i : b + 8 * i + 8, B * t : B * t + B] for t in range(2) for i in range(u, nt)
            }
            C = {
                (i, j): jnp.broadcast_to(T[i, 0][:, cb + j : cb + j + 1], (8, B))
                for i in range(u, nt)
                for j in range(8)
            }
            sc = jnp.ones((8, B), F32)
            for j in range(8):
                piv = jnp.broadcast_to(C[u, j][j : j + 1, :], (8, B))
                inv = 1.0 / piv
                sc = jnp.where(sub == j, lax.rsqrt(piv), sc)
                rows = [jnp.broadcast_to(T[u, t][j : j + 1, :], (8, B)) for t in range(2)]
                cs = {jj: jnp.broadcast_to(C[u, jj][j : j + 1, :], (8, B)) for jj in range(j + 1, 8)}
                for i in range(u, nt):
                    m = C[i, j] * inv
                    if i == u:
                        if j == 7:
                            continue
                        m = jnp.where(sub > j, m, 0.0)
                    for jj in range(j + 1, 8):
                        C[i, jj] = C[i, jj] - m * cs[jj]
                    for t in range(2):
                        T[i, t] = T[i, t] - m * rows[t]
            for t in range(2):
                T[u, t] = T[u, t] * sc
            for (i, t), v in T.items():
                m2[b + 8 * i : b + 8 * i + 8, B * t : B * t + B] = v
            yield
        if b + NB < B:
            R = m2[b : b + NB, :]
            g = lax.dot_general(
                R[:, b + NB : B], R, (((0,), (0,)), ((), ())), precision=HIGH, preferred_element_type=F32
            )
            m2[b + NB : B, :] = m2[b + NB : B, :] - g
            yield


def factor_lead(lead, m2, s, e, diag, arrived):
    n = 4
    ri = lax.broadcasted_iota(jnp.int32, (B, B), 0)
    ci = lax.broadcasted_iota(jnp.int32, (B, B), 1)
    e[...] = jnp.zeros_like(e)
    for k in range(n):
        a, z = B * k, B * k + B
        if k == 0:
            arrived(0)
            m2[:, :B] = lead[0, 0]
        else:
            m2[:, :B] = s[a:z, a:z]
        m2[:, B:] = jnp.where(ri == ci, 1.0, 0.0).astype(F32)
        yield from eliminate(m2)
        if k == 0:
            for i in range(1, n):
                arrived(i)
                s[B * i : B * i + B, B * i : B * i + B] = lead[i, i]
                for kk in range(i):
                    s[B * kk : B * kk + B, B * i : B * i + B] = lead[i, kk].T
            yield
        li = jnp.where(ri >= ci, m2[:, B:], 0.0)
        diag[k] = jnp.where(ri >= ci, m2[:, :B].T, 0.0)
        parts = []
        if k < n - 1:
            parts.append(s[a:z, z:])
        if k > 0:
            parts.append(e[a:z, :a])
        R = jnp.dot(li, jnp.concatenate(parts, axis=1), precision=HIGH, preferred_element_type=F32)
        w = (n - 1 - k) * B
        if k > 0:
            e[a:z, :a] = R[:, w:]
        e[a:z, a:z] = li
        if k < n - 1:
            s[a:z, z:] = R[:, :w]
            yield
            full = jnp.concatenate([s[a:z, z:], e[a:z, :z]], axis=1)
            g = lax.dot_general(
                full[:, :w], full, (((0,), (0,)), ((), ())), precision=HIGH, preferred_element_type=F32
            )
            s[z:, z:] = s[z:, z:] - g[:, :w]
            e[z:, :z] = e[z:, :z] - g[:, w:]
        yield


def split(v):
    hi = v.astype(BF16)
    return hi, (v - hi.astype(F32)).astype(BF16)


def dot_nt(a, b):
    (ah, al), (bh, bl) = a, b
    mm = lambda p, q: lax.dot_general(p, q, (((1,), (1,)), ((), ())), preferred_element_type=F32)
    return mm(ah, bh) + (mm(ah, bl) + mm(al, bh))


def finish_kernel(
    ids, coupled, values, left, right, inverse, diag, out,
    obuf, ehi, elo, whi, wlo, g, osem,
):
    r = lax.axis_index("row")
    hi, lo = split(inverse[...])
    ehi[...] = hi
    elo[...] = lo

    def factor_rows(blocks):
        cat = [blocks[k].reshape(4 * B, B) for k in range(4)]
        parts = [split(c) for c in cat]
        xh = jnp.concatenate([p[0] for p in parts], axis=1)
        xl = jnp.concatenate([p[1] for p in parts], axis=1)
        h = 2 * B
        w0 = dot_nt((xh[:, :h], xl[:, :h]), (ehi[:h, :h], elo[:h, :h]))
        w1 = dot_nt((xh, xl), (ehi[h:, :], elo[h:, :]))
        return jnp.concatenate([w0, w1], axis=1)

    wl = factor_rows(left)
    for n in range(4):
        for a in range(4):
            g[64 + 4 * n + a] = -wl[B * a : B * a + B, B * n : B * n + B]
    g[80] = jnp.zeros((B, B), F32)

    @pl.when(r < 4)
    def _():
        g[64 + 4 * r] = -diag[r]

    hi, lo = split(wl)
    whi[...] = hi
    wlo[...] = lo

    @pl.loop(0, 4)
    def _(y):
        wr = factor_rows(right.at[y])
        p = dot_nt((whi[...], wlo[...]), split(wr))
        for b in range(4):
            for a in range(4):
                g[(y * 4 + b) * 4 + a] = p[B * a : B * a + B, B * b : B * b + B]

    @pl.loop(0, SLOTS)
    def _(slot):
        i = ids[0, slot]
        j = ids[1, slot]
        a = jnp.int32(0)
        own = jnp.int32(0)
        b = jnp.int32(0)
        r2 = j & 31
        for n in range(4):
            hit = i == coupled[n, r]
            a = jnp.where(hit, n, a)
            own = jnp.where(hit, 1, own)
            b = jnp.where(j == coupled[n, r2], n, b)
        found = own == 1
        trailing = found & (j >= 4)
        panel = found & (j < 4)
        place = jnp.where(trailing, ((r2 // 8) * 4 + b) * 4 + a, jnp.where(panel, 64 + 4 * j + a, 80))
        keep = (i >= 0) & jnp.logical_not(panel)
        obuf[slot] = jnp.where(keep, values[slot], 0.0) - g[place]
        pltpu.make_async_copy(obuf.at[slot], out.at[slot], osem).start()

    pltpu.make_async_copy(obuf, out, osem).wait()


def finish(ids, coupled, values, left, right, inverse, diag):
    smem = pl.BlockSpec(memory_space=pltpu.SMEM)
    vmem = pl.BlockSpec(memory_space=pltpu.VMEM)
    hbm = pl.BlockSpec(memory_space=pltpu.HBM)
    dma = pltpu.SemaphoreType.DMA
    return pl.pallas_call(
        finish_kernel,
        out_shape=jax.ShapeDtypeStruct((SLOTS, B, B), F32),
        in_specs=[smem, smem, vmem, vmem, vmem, vmem, vmem],
        out_specs=hbm,
        scratch_shapes=[
            pltpu.VMEM((SLOTS, B, B), F32),
            pltpu.VMEM((512, 512), BF16),
            pltpu.VMEM((512, 512), BF16),
            pltpu.VMEM((512, 512), BF16),
            pltpu.VMEM((512, 512), BF16),
            pltpu.VMEM((81, B, B), F32),
            dma,
        ],
        compiler_params=pltpu.CompilerParams(vmem_limit_bytes=32 << 20),
        name="finish",
    )(ids, coupled, values, left, right, inverse, diag)


def body(values, block_ids, coupled_rows):
    ids = block_ids[0, 0].T
    coupled = coupled_rows.T
    left, right, inverse, diag = exchange(ids, coupled, values[0, 0])
    out = finish(ids, coupled, values[0, 0], left, right, inverse, diag)
    return out[None, None]


def solution(mesh):
    placed = (P("row", "col", None, None, None), P("row", "col", None, None), P())
    return jax.shard_map(
        body,
        mesh=mesh,
        in_specs=placed,
        out_specs=P("row", "col", None, None, None),
        check_vma=False,
    )
```

```python
import jax
import jax.numpy as jnp
from jax import lax
from jax.experimental import pallas as pl
from jax.experimental.pallas import tpu as pltpu
from jax.sharding import PartitionSpec as P

B = 128
NB = 32
SLOTS = 68
HIGH = lax.Precision.HIGHEST
MESH = pl.DeviceIdType.MESH
F32 = jnp.float32
BF16 = jnp.bfloat16


def exchange_kernel(
    ids, coupled, values, left, right, inverse, diag, vbuf, lead, m2, s, vsem,
    zus, zds, zr, xs, xr, os_, ys, yr, yfs, yfr, ss, sr, fr, f1s, f2s, f3s, f4s,
    g0s, g0r, g1s, g1r, g2s, g2r, g3s, g3r, g4s, g4r,
):
    r = lax.axis_index("row")
    z = lax.axis_index("col")
    h = lax.rem(r, 2)
    x = lax.rem(r // 2, 4)
    y = r // 8
    up = lax.rem(z + 1, 8)
    down = lax.rem(z + 7, 8)
    sib = r + 1 - 2 * h
    xo = [y * 8 + lax.rem(x + d, 4) * 2 + h for d in (1, 3, 2)]
    yo = [lax.rem(y + d, 4) * 8 + x * 2 + h for d in (1, 3, 2)]
    origin = x == z // 2
    source = origin & (h == lax.rem(z, 2))
    true = r >= 0

    load = pltpu.make_async_copy(values, vbuf, vsem)
    pl.when(z < 4)(load.start)

    barrier = pltpu.get_barrier_semaphore()

    def greet(row, col):
        pl.semaphore_signal(barrier, inc=1, device_id={"row": row, "col": col}, device_id_type=MESH)

    for d in range(1, 8):
        greet(r, lax.rem(z + d, 8))
    for d in range(1, 16):
        greet(lax.rem(r + 2 * d, 32), z)
    greet(sib, z)

    def scan(slot, found):
        i = ids[0, slot]
        hit = ids[1, slot] == z
        return tuple(jnp.where(hit & (i == coupled[a, r]), slot, found[a]) for a in range(4))

    found = lax.fori_loop(0, SLOTS, scan, (jnp.int32(-1),) * 4)
    pl.semaphore_wait(barrier, 23)

    @pl.when(z < 4)
    def _():
        load.wait()
        for a in range(4):
            block = vbuf[jnp.maximum(found[a], 0)]
            left[z, a] = jnp.where(found[a] >= 0, block, 0.0)

    def copy(src, dst, ssem, rsem, row, col):
        return pltpu.make_async_remote_copy(
            src_ref=src, dst_ref=dst, send_sem=ssem, recv_sem=rsem,
            device_id={"row": row, "col": col}, device_id_type=MESH,
        )

    sends = []

    def send(cond, desc):
        pl.when(cond)(desc.start)
        sends.append((cond, desc))

    half = pl.ds(2 * h, 2)
    other = pl.ds(2 - 2 * h, 2)

    def travellers(d):
        if d == 0:
            return [(jnp.minimum(z, 3), z < 4, true, true)]
        ku = lax.rem(z + 8 - d, 8)
        reach = jnp.where(ku >= 2, 5, 2)
        kd = lax.rem(z + d, 8)
        depth = jnp.where(kd >= 2, 2, 5)
        return [
            (jnp.minimum(ku, 3), (ku <= 3) & (d <= reach), d < reach, None),
            (jnp.minimum(kd, 3), (kd <= 3) & (d <= depth), None, d < depth),
        ]

    def spread(k, cond):
        block = right.at[y, k, half]
        for n in range(2):
            send(cond, copy(block, block, ys.at[k, n], yr.at[y, k], yo[n], z))
        send(cond, copy(block, block, ss.at[y, k], sr.at[y, k], sib, z))

    def spread_x(k, cond):
        block = right.at[y, k, half]
        for n in range(3):
            send(cond & origin, copy(block, block, xs.at[k, n], xr.at[k], xo[n], z))

    def z_event(d):
        for k, valid, go_up, go_down in travellers(d):
            for a in range(4):
                block = left.at[k, a]
                if d > 0:
                    pl.when(valid)(copy(block, block, zus.at[k, a], zr.at[k, a], r, up).wait_recv)
                if go_up is not None:
                    send(valid & go_up, copy(block, block, zus.at[k, a], zr.at[k, a], r, up))
                if go_down is not None:
                    send(valid & go_down, copy(block, block, zds.at[k, a], zr.at[k, a], r, down))
            mine = valid & source

            @pl.when(mine)
            def _():
                right[y, k, half] = left[k, half]

            send(mine, copy(left.at[k, other], right.at[y, k, other], os_.at[k], xr.at[k], sib, z))
            spread_x(k, mine)
            spread(k, mine)

    def x_event(d):
        for k, valid, _, _ in travellers(d):
            block = right.at[y, k, half]
            mine = valid & jnp.logical_not(source)
            pl.when(mine)(copy(block, block, os_.at[k], xr.at[k], sib, z).wait_recv)
            spread_x(k, mine)
            spread(k, mine)

    def y_event(d, n):
        yy = lax.rem(y + (1, 3, 2)[n], 4)
        for k, valid, _, _ in travellers(d):
            block = right.at[yy, k, half]
            if n < 2:
                pl.when(valid)(copy(block, block, ys.at[k, n], yr.at[yy, k], yo[n], z).wait_recv)
                q = 1 - n
                part = right.at[yy, k, 2 * h + q]
                send(valid, copy(part, part, yfs.at[k, q], yfr.at[k, q], yo[1 - n], z))
            else:
                for q in range(2):
                    part = right.at[yy, k, 2 * h + q]
                    pl.when(valid)(copy(part, part, yfs.at[k, q], yfr.at[k, q], yo[q], z).wait_recv)
            send(valid, copy(block, block, ss.at[yy, k], sr.at[yy, k], sib, z))

    first = lead.at[0, 4]

    def first_z():
        mine = (r == 0) & (z == 0)

        @pl.when(mine)
        def _():
            lead[0, 4] = left[0, 0]

        for d in range(1, 8):
            send(mine, copy(first, first, f1s.at[d - 1], fr, r, lax.rem(z + d, 8)))

    def first_out(mine):
        for n in range(3):
            send(mine, copy(first, first, f3s.at[n], fr, xo[n], z))
        send(mine, copy(first, first, f4s, fr, sib, z))

    def first_y():
        mine = r == 0
        pl.when(mine & (z != 0))(copy(first, first, f4s, fr, sib, z).wait_recv)
        for n in range(3):
            send(mine, copy(first, first, f2s.at[n], fr, yo[n], z))
        first_out(mine)

    def first_x():
        mine = (h == 0) & (x == 0) & (y > 0)
        pl.when(mine)(copy(first, first, f4s, fr, sib, z).wait_recv)
        first_out(mine)

    def first_s():
        mine = (h == 0) & (x > 0)
        pl.when(mine)(copy(first, first, f4s, fr, sib, z).wait_recv)
        send(mine, copy(first, first, f4s, fr, sib, z))

    rows = lambda yy, xx: pl.ds(pl.multiple_of(32 * yy + 8 * xx, 8), 8)
    mine8 = rows(y, x)
    zc = jnp.minimum(z, 3)

    def here(j, k):
        i = 2 * j + h
        return (i >= k) & (i > 0)

    def slot_of(j, k):
        return k if j else 4 + jnp.minimum(k, 1)

    def lead_scatter():
        for j in range(2):
            mine = (r == 2 * j + h) & (z < 4) & here(j, z)
            slot = slot_of(j, zc)

            @pl.when(mine)
            def _():
                lead[h, slot, mine8] = left[zc, 0, mine8]

            for d in range(1, 16):
                p = lax.rem(y * 4 + x + d, 16)
                at = rows(p // 4, lax.rem(p, 4))
                part, target = left.at[zc, 0, at], lead.at[h, slot, at]
                send(mine, copy(part, target, g0s.at[d - 1], g0r.at[j], p * 2 + h, z))

    def lead_planes():
        @pl.when(h == 0)
        def _():
            lead[0, 5, mine8] = jnp.zeros((8, B), F32)
            lead[0, 3, mine8] = jnp.zeros((8, B), F32)

        for j in range(2):
            mine = (z < 4) & here(j, z)
            part = lead.at[h, slot_of(j, zc), mine8]
            pl.when(mine & (r != 2 * j + h))(copy(part, part, g0s.at[0], g0r.at[j], sib, z).wait_recv)
            for d in range(1, 8):
                send(mine, copy(part, part, g1s.at[j, d - 1], g1r.at[j, zc], r, lax.rem(z + d, 8)))

    def lead_x():
        for j in range(2):
            for k in range(4 if j else 2):
                part = lead.at[h, slot_of(j, k), mine8]
                pl.when(here(j, k) & (z != k))(copy(part, part, g1s.at[j, 0], g1r.at[j, k], r, up).wait_recv)
        for first_slot, count in ((0, 4), (4, 2)):
            q = first_slot // 4
            part = lead.at[h, pl.ds(first_slot, count), mine8]
            for n in range(3):
                send(true, copy(part, part, g2s.at[q, n], g2r.at[q, x], xo[n], z)) if q == 0 else send(
                    h == 1, copy(part, part, g2s.at[q, n], g2r.at[q, x], xo[n], z)
                )

    def lead_y():
        for first_slot, count in ((0, 4), (4, 2)):
            q = first_slot // 4
            for d in (1, 3, 2):
                xx = lax.rem(x + d, 4)
                part = lead.at[h, pl.ds(first_slot, count), rows(y, xx)]
                pl.when((h == 1) | (q == 0))(copy(part, part, g2s.at[q, 0], g2r.at[q, xx], sib, z).wait_recv)
            part = lead.at[h, pl.ds(first_slot, count), pl.ds(pl.multiple_of(32 * y, 32), 32)]
            for n in range(3):
                send((h == 1) | (q == 0), copy(part, part, g3s.at[q, n], g3r.at[q, y], yo[n], z))

    def lead_s():
        for first_slot, count in ((0, 4), (4, 2)):
            q = first_slot // 4
            for d in (1, 3, 2):
                yy = lax.rem(y + d, 4)
                part = lead.at[h, pl.ds(first_slot, count), pl.ds(pl.multiple_of(32 * yy, 32), 32)]
                pl.when((h == 1) | (q == 0))(copy(part, part, g3s.at[q, 0], g3r.at[q, yy], sib, z).wait_recv)
            part = lead.at[h, pl.ds(first_slot, count)]
            send((h == 1) | (q == 0), copy(part, part, g4s.at[q], g4r.at[q], sib, z))

    def lead_arrived(i):
        if i == 0:
            pl.when(h == 1)(copy(first, first, f4s, fr, sib, z).wait_recv)
        if i == 1:
            part = lead.at[1 - h, pl.ds(0, 4)]
            copy(part, part, g4s.at[0], g4r.at[0], sib, z).wait_recv()
            part = lead.at[1 - h, pl.ds(4, 2)]
            pl.when(h == 0)(copy(part, part, g4s.at[1], g4r.at[1], sib, z).wait_recv)

    steps = factor_lead(lead, m2, s, inverse, diag, lead_arrived)

    def work(count):
        for _ in range(count):
            next(steps, None)

    first_z()
    lead_scatter()
    z_event(0)
    lead_planes()
    z_event(1)
    first_y()
    x_event(0)
    z_event(2)
    first_x()
    lead_x()
    x_event(1)
    for n in range(3):
        y_event(0, n)
    z_event(3)
    first_s()
    lead_y()
    work(4)
    x_event(2)
    for n in range(3):
        work(4)
        y_event(1, n)
    lead_s()
    z_event(4)
    work(4)
    x_event(3)
    for n in range(3):
        work(4)
        y_event(2, n)
    z_event(5)
    work(4)
    x_event(4)
    for n in range(3):
        work(4)
        y_event(3, n)
    work(4)
    x_event(5)
    for n in range(3):
        work(4)
        y_event(4, n)
    for n in range(3):
        work(4)
        y_event(5, n)
    for _ in steps:
        pass

    for yy in range(4):
        for k in range(4):
            block = right.at[yy, k, other]
            copy(block, block, ss.at[yy, k], sr.at[yy, k], sib, z).wait_recv()
    for cond, desc in sends:
        pl.when(cond)(desc.wait_send)


def exchange(ids, coupled, values):
    dma = pltpu.SemaphoreType.DMA
    vmem = pl.BlockSpec(memory_space=pltpu.VMEM)
    return pl.pallas_call(
        exchange_kernel,
        out_shape=(
            jax.ShapeDtypeStruct((4, 4, B, B), F32),
            jax.ShapeDtypeStruct((4, 4, 4, B, B), F32),
            jax.ShapeDtypeStruct((512, 512), F32),
            jax.ShapeDtypeStruct((4, B, B), F32),
        ),
        in_specs=[
            pl.BlockSpec(memory_space=pltpu.SMEM),
            pl.BlockSpec(memory_space=pltpu.SMEM),
            pl.BlockSpec(memory_space=pltpu.HBM),
        ],
        out_specs=(vmem, vmem, vmem, vmem),
        scratch_shapes=[
            pltpu.VMEM((SLOTS, B, B), F32),
            pltpu.VMEM((2, 6, B, B), F32),
            pltpu.VMEM((B, 2 * B), F32),
            pltpu.VMEM((512, 512), F32),
            dma,
            dma((4, 4)), dma((4, 4)), dma((4, 4)),
            dma((4, 3)), dma((4,)), dma((4,)),
            dma((4, 2)), dma((4, 4)), dma((4, 2)), dma((4, 2)),
            dma((4, 4)), dma((4, 4)),
            dma, dma((7,)), dma((3,)), dma((3,)), dma,
            dma((15,)), dma((2,)),
            dma((2, 7)), dma((2, 4)),
            dma((2, 3)), dma((2, 4)),
            dma((2, 3)), dma((2, 4)),
            dma((2,)), dma((2,)),
        ],
        compiler_params=pltpu.CompilerParams(
            collective_id=0, has_side_effects=True, vmem_limit_bytes=46 << 20
        ),
        name="exchange",
    )(ids, coupled, values)


def eliminate(m2):
    sub = lax.broadcasted_iota(jnp.int32, (8, B), 0)
    nt = NB // 8
    for p in range(B // NB):
        b = NB * p
        for u in range(nt):
            cb = b + 8 * u
            T = {
                (i, t): m2[b + 8 * i : b + 8 * i + 8, B * t : B * t + B] for t in range(2) for i in range(u, nt)
            }
            C = {
                (i, j): jnp.broadcast_to(T[i, 0][:, cb + j : cb + j + 1], (8, B))
                for i in range(u, nt)
                for j in range(8)
            }
            sc = jnp.ones((8, B), F32)
            for j in range(8):
                piv = jnp.broadcast_to(C[u, j][j : j + 1, :], (8, B))
                inv = 1.0 / piv
                sc = jnp.where(sub == j, lax.rsqrt(piv), sc)
                rows = [jnp.broadcast_to(T[u, t][j : j + 1, :], (8, B)) for t in range(2)]
                cs = {jj: jnp.broadcast_to(C[u, jj][j : j + 1, :], (8, B)) for jj in range(j + 1, 8)}
                for i in range(u, nt):
                    m = C[i, j] * inv
                    if i == u:
                        if j == 7:
                            continue
                        m = jnp.where(sub > j, m, 0.0)
                    for jj in range(j + 1, 8):
                        C[i, jj] = C[i, jj] - m * cs[jj]
                    for t in range(2):
                        T[i, t] = T[i, t] - m * rows[t]
            for t in range(2):
                T[u, t] = T[u, t] * sc
            for (i, t), v in T.items():
                m2[b + 8 * i : b + 8 * i + 8, B * t : B * t + B] = v
            yield
        if b + NB < B:
            R = m2[b : b + NB, :]
            g = lax.dot_general(
                R[:, b + NB : B], R, (((0,), (0,)), ((), ())), precision=HIGH, preferred_element_type=F32
            )
            m2[b + NB : B, :] = m2[b + NB : B, :] - g
            yield


def factor_lead(lead, m2, s, e, diag, arrived):
    n = 4
    ri = lax.broadcasted_iota(jnp.int32, (B, B), 0)
    ci = lax.broadcasted_iota(jnp.int32, (B, B), 1)
    e[...] = jnp.zeros_like(e)
    for k in range(n):
        a, z = B * k, B * k + B
        if k == 0:
            arrived(0)
            m2[:, :B] = lead[0, 4]
        else:
            m2[:, :B] = s[a:z, a:z]
        m2[:, B:] = jnp.where(ri == ci, 1.0, 0.0).astype(F32)
        yield from eliminate(m2)
        if k == 0:
            for i in range(1, n):
                arrived(i)
                base = 4 if i < 2 else 0
                s[B * i : B * i + B, B * i : B * i + B] = lead[i % 2, base + i]
                for kk in range(i):
                    s[B * kk : B * kk + B, B * i : B * i + B] = lead[i % 2, base + kk].T
            yield
        li = jnp.where(ri >= ci, m2[:, B:], 0.0)
        diag[k] = jnp.where(ri >= ci, m2[:, :B].T, 0.0)
        parts = []
        if k < n - 1:
            parts.append(s[a:z, z:])
        if k > 0:
            parts.append(e[a:z, :a])
        R = jnp.dot(li, jnp.concatenate(parts, axis=1), precision=HIGH, preferred_element_type=F32)
        w = (n - 1 - k) * B
        if k > 0:
            e[a:z, :a] = R[:, w:]
        e[a:z, a:z] = li
        if k < n - 1:
            s[a:z, z:] = R[:, :w]
            yield
            full = jnp.concatenate([s[a:z, z:], e[a:z, :z]], axis=1)
            g = lax.dot_general(
                full[:, :w], full, (((0,), (0,)), ((), ())), precision=HIGH, preferred_element_type=F32
            )
            s[z:, z:] = s[z:, z:] - g[:, :w]
            e[z:, :z] = e[z:, :z] - g[:, w:]
        yield


def split(v):
    hi = v.astype(BF16)
    return hi, (v - hi.astype(F32)).astype(BF16)


def dot_nt(a, b):
    (ah, al), (bh, bl) = a, b
    mm = lambda p, q: lax.dot_general(p, q, (((1,), (1,)), ((), ())), preferred_element_type=F32)
    return mm(ah, bh) + (mm(ah, bl) + mm(al, bh))


def finish_kernel(
    ids, coupled, values, left, right, inverse, diag, out,
    obuf, ehi, elo, whi, wlo, g, osem,
):
    r = lax.axis_index("row")
    hi, lo = split(inverse[...])
    ehi[...] = hi
    elo[...] = lo

    def factor_rows(blocks):
        cat = [blocks[k].reshape(4 * B, B) for k in range(4)]
        parts = [split(c) for c in cat]
        xh = jnp.concatenate([p[0] for p in parts], axis=1)
        xl = jnp.concatenate([p[1] for p in parts], axis=1)
        h = 2 * B
        w0 = dot_nt((xh[:, :h], xl[:, :h]), (ehi[:h, :h], elo[:h, :h]))
        w1 = dot_nt((xh, xl), (ehi[h:, :], elo[h:, :]))
        return jnp.concatenate([w0, w1], axis=1)

    wl = factor_rows(left)
    for n in range(4):
        for a in range(4):
            g[64 + 4 * n + a] = -wl[B * a : B * a + B, B * n : B * n + B]
    g[80] = jnp.zeros((B, B), F32)

    @pl.when(r < 4)
    def _():
        g[64 + 4 * r] = -diag[r]

    hi, lo = split(wl)
    whi[...] = hi
    wlo[...] = lo

    @pl.loop(0, 4)
    def _(y):
        wr = factor_rows(right.at[y])
        p = dot_nt((whi[...], wlo[...]), split(wr))
        for b in range(4):
            for a in range(4):
                g[(y * 4 + b) * 4 + a] = p[B * a : B * a + B, B * b : B * b + B]

    @pl.loop(0, SLOTS)
    def _(slot):
        i = ids[0, slot]
        j = ids[1, slot]
        a = jnp.int32(0)
        own = jnp.int32(0)
        b = jnp.int32(0)
        r2 = j & 31
        for n in range(4):
            hit = i == coupled[n, r]
            a = jnp.where(hit, n, a)
            own = jnp.where(hit, 1, own)
            b = jnp.where(j == coupled[n, r2], n, b)
        found = own == 1
        trailing = found & (j >= 4)
        panel = found & (j < 4)
        place = jnp.where(trailing, ((r2 // 8) * 4 + b) * 4 + a, jnp.where(panel, 64 + 4 * j + a, 80))
        keep = (i >= 0) & jnp.logical_not(panel)
        obuf[slot] = jnp.where(keep, values[slot], 0.0) - g[place]
        pltpu.make_async_copy(obuf.at[slot], out.at[slot], osem).start()

    pltpu.make_async_copy(obuf, out, osem).wait()


def finish(ids, coupled, values, left, right, inverse, diag):
    smem = pl.BlockSpec(memory_space=pltpu.SMEM)
    vmem = pl.BlockSpec(memory_space=pltpu.VMEM)
    hbm = pl.BlockSpec(memory_space=pltpu.HBM)
    dma = pltpu.SemaphoreType.DMA
    return pl.pallas_call(
        finish_kernel,
        out_shape=jax.ShapeDtypeStruct((SLOTS, B, B), F32),
        in_specs=[smem, smem, vmem, vmem, vmem, vmem, vmem],
        out_specs=hbm,
        scratch_shapes=[
            pltpu.VMEM((SLOTS, B, B), F32),
            pltpu.VMEM((512, 512), BF16),
            pltpu.VMEM((512, 512), BF16),
            pltpu.VMEM((512, 512), BF16),
            pltpu.VMEM((512, 512), BF16),
            pltpu.VMEM((81, B, B), F32),
            dma,
        ],
        compiler_params=pltpu.CompilerParams(vmem_limit_bytes=32 << 20),
        name="finish",
    )(ids, coupled, values, left, right, inverse, diag)


def body(values, block_ids, coupled_rows):
    ids = block_ids[0, 0].T
    coupled = coupled_rows.T
    left, right, inverse, diag = exchange(ids, coupled, values[0, 0])
    out = finish(ids, coupled, values[0, 0], left, right, inverse, diag)
    return out[None, None]


def solution(mesh):
    placed = (P("row", "col", None, None, None), P("row", "col", None, None), P())
    return jax.shard_map(
        body,
        mesh=mesh,
        in_specs=placed,
        out_specs=P("row", "col", None, None, None),
        check_vma=False,
    )
```

```python
import jax
import jax.numpy as jnp
from jax import lax
from jax.experimental import pallas as pl
from jax.experimental.pallas import tpu as pltpu
from jax.sharding import PartitionSpec as P

B = 128
NB = 32
SLOTS = 68
HIGH = lax.Precision.HIGHEST
MESH = pl.DeviceIdType.MESH
F32 = jnp.float32
BF16 = jnp.bfloat16


def exchange_kernel(
    ids, coupled, values, left, right, inverse, diag, vbuf, lead, m2, s, vsem,
    zus, zds, zr, xs, xr, os_, ys, yr, yfs, yfr, ss, sr, fr, f1s, f2s, f3s, f4s,
    g0s, g0r, g1s, g1r, g2s, g2r, g3s, g3r, g4s, g4r,
):
    r = lax.axis_index("row")
    z = lax.axis_index("col")
    h = lax.rem(r, 2)
    x = lax.rem(r // 2, 4)
    y = r // 8
    up = lax.rem(z + 1, 8)
    down = lax.rem(z + 7, 8)
    sib = r + 1 - 2 * h
    xo = [y * 8 + lax.rem(x + d, 4) * 2 + h for d in (1, 3, 2)]
    yo = [lax.rem(y + d, 4) * 8 + x * 2 + h for d in (1, 3, 2)]
    origin = x == z // 2
    source = origin & (h == lax.rem(z, 2))
    true = r >= 0

    load = pltpu.make_async_copy(values, vbuf, vsem)
    pl.when(z < 4)(load.start)

    barrier = pltpu.get_barrier_semaphore()

    def greet(row, col):
        pl.semaphore_signal(barrier, inc=1, device_id={"row": row, "col": col}, device_id_type=MESH)

    for d in range(1, 8):
        greet(r, lax.rem(z + d, 8))
    for d in range(1, 16):
        greet(lax.rem(r + 2 * d, 32), z)
    greet(sib, z)

    def scan(slot, found):
        i = ids[0, slot]
        hit = ids[1, slot] == z
        return tuple(jnp.where(hit & (i == coupled[a, r]), slot, found[a]) for a in range(4))

    found = lax.fori_loop(0, SLOTS, scan, (jnp.int32(-1),) * 4)
    pl.semaphore_wait(barrier, 23)

    @pl.when(z < 4)
    def _():
        load.wait()
        for a in range(4):
            block = vbuf[jnp.maximum(found[a], 0)]
            left[z, a] = jnp.where(found[a] >= 0, block, 0.0)

    def copy(src, dst, ssem, rsem, row, col):
        return pltpu.make_async_remote_copy(
            src_ref=src, dst_ref=dst, send_sem=ssem, recv_sem=rsem,
            device_id={"row": row, "col": col}, device_id_type=MESH,
        )

    sends = []

    def send(cond, desc):
        pl.when(cond)(desc.start)
        sends.append((cond, desc))

    half = pl.ds(2 * h, 2)
    other = pl.ds(2 - 2 * h, 2)

    def travellers(d):
        if d == 0:
            return [(jnp.minimum(z, 3), z < 4, true, true)]
        ku = lax.rem(z + 8 - d, 8)
        reach = jnp.where(ku >= 2, 5, 2)
        kd = lax.rem(z + d, 8)
        depth = jnp.where(kd >= 2, 2, 5)
        return [
            (jnp.minimum(ku, 3), (ku <= 3) & (d <= reach), d < reach, None),
            (jnp.minimum(kd, 3), (kd <= 3) & (d <= depth), None, d < depth),
        ]

    def spread(k, cond):
        block = right.at[y, k, half]
        for n in range(2):
            send(cond, copy(block, block, ys.at[k, n], yr.at[y, k], yo[n], z))
        send(cond, copy(block, block, ss.at[y, k], sr.at[y, k], sib, z))

    def spread_x(k, cond):
        block = right.at[y, k, half]
        for n in range(3):
            send(cond & origin, copy(block, block, xs.at[k, n], xr.at[k], xo[n], z))

    def z_event(d):
        group = travellers(d)
        for a in range(4):
            for k, valid, go_up, go_down in group:
                block = left.at[k, a]
                if d > 0:
                    pl.when(valid)(copy(block, block, zus.at[k, a], zr.at[k, a], r, up).wait_recv)
                if go_up is not None:
                    send(valid & go_up, copy(block, block, zus.at[k, a], zr.at[k, a], r, up))
                if go_down is not None:
                    send(valid & go_down, copy(block, block, zds.at[k, a], zr.at[k, a], r, down))
        for k, valid, _, _ in group:
            mine = valid & source

            @pl.when(mine)
            def _():
                right[y, k, half] = left[k, half]

            send(mine, copy(left.at[k, other], right.at[y, k, other], os_.at[k], xr.at[k], sib, z))
            spread_x(k, mine)
            spread(k, mine)

    def x_event(d):
        for k, valid, _, _ in travellers(d):
            block = right.at[y, k, half]
            mine = valid & jnp.logical_not(source)
            pl.when(mine)(copy(block, block, os_.at[k], xr.at[k], sib, z).wait_recv)
            spread_x(k, mine)
            spread(k, mine)

    def y_event(d, n):
        yy = lax.rem(y + (1, 3, 2)[n], 4)
        for k, valid, _, _ in travellers(d):
            block = right.at[yy, k, half]
            if n < 2:
                pl.when(valid)(copy(block, block, ys.at[k, n], yr.at[yy, k], yo[n], z).wait_recv)
                q = 1 - n
                part = right.at[yy, k, 2 * h + q]
                send(valid, copy(part, part, yfs.at[k, q], yfr.at[k, q], yo[1 - n], z))
            else:
                for q in range(2):
                    part = right.at[yy, k, 2 * h + q]
                    pl.when(valid)(copy(part, part, yfs.at[k, q], yfr.at[k, q], yo[q], z).wait_recv)
            send(valid, copy(block, block, ss.at[yy, k], sr.at[yy, k], sib, z))

    first = lead.at[0, 4]

    def first_z():
        mine = (r == 0) & (z == 0)

        @pl.when(mine)
        def _():
            lead[0, 4] = left[0, 0]

        for d in range(1, 8):
            send(mine, copy(first, first, f1s.at[d - 1], fr, r, lax.rem(z + d, 8)))

    def first_out(mine):
        for n in range(3):
            send(mine, copy(first, first, f3s.at[n], fr, xo[n], z))
        send(mine, copy(first, first, f4s, fr, sib, z))

    def first_y():
        mine = r == 0
        pl.when(mine & (z != 0))(copy(first, first, f4s, fr, sib, z).wait_recv)
        for n in range(3):
            send(mine, copy(first, first, f2s.at[n], fr, yo[n], z))
        first_out(mine)

    def first_x():
        mine = (h == 0) & (x == 0) & (y > 0)
        pl.when(mine)(copy(first, first, f4s, fr, sib, z).wait_recv)
        first_out(mine)

    def first_s():
        mine = (h == 0) & (x > 0)
        pl.when(mine)(copy(first, first, f4s, fr, sib, z).wait_recv)
        send(mine, copy(first, first, f4s, fr, sib, z))

    rows = lambda yy, xx: pl.ds(pl.multiple_of(32 * yy + 8 * xx, 8), 8)
    mine8 = rows(y, x)
    zc = jnp.minimum(z, 3)

    def here(j, k):
        i = 2 * j + h
        return (i >= k) & (i > 0)

    def slot_of(j, k):
        return k if j else 4 + jnp.minimum(k, 1)

    def lead_scatter():
        for j in range(2):
            mine = (r == 2 * j + h) & (z < 4) & here(j, z)
            slot = slot_of(j, zc)

            @pl.when(mine)
            def _():
                lead[h, slot, mine8] = left[zc, 0, mine8]

            for d in range(1, 16):
                p = lax.rem(y * 4 + x + d, 16)
                at = rows(p // 4, lax.rem(p, 4))
                part, target = left.at[zc, 0, at], lead.at[h, slot, at]
                send(mine, copy(part, target, g0s.at[d - 1], g0r.at[j], p * 2 + h, z))

    def lead_planes():
        @pl.when(h == 0)
        def _():
            lead[0, 5, mine8] = jnp.zeros((8, B), F32)
            lead[0, 3, mine8] = jnp.zeros((8, B), F32)

        for j in range(2):
            mine = (z < 4) & here(j, z)
            part = lead.at[h, slot_of(j, zc), mine8]
            pl.when(mine & (r != 2 * j + h))(copy(part, part, g0s.at[0], g0r.at[j], sib, z).wait_recv)
            for d in range(1, 8):
                send(mine, copy(part, part, g1s.at[j, d - 1], g1r.at[j, zc], r, lax.rem(z + d, 8)))

    def lead_x():
        for j in range(2):
            for k in range(4 if j else 2):
                part = lead.at[h, slot_of(j, k), mine8]
                pl.when(here(j, k) & (z != k))(copy(part, part, g1s.at[j, 0], g1r.at[j, k], r, up).wait_recv)
        for first_slot, count in ((0, 4), (4, 2)):
            q = first_slot // 4
            part = lead.at[h, pl.ds(first_slot, count), mine8]
            for n in range(3):
                send(true, copy(part, part, g2s.at[q, n], g2r.at[q, x], xo[n], z)) if q == 0 else send(
                    h == 1, copy(part, part, g2s.at[q, n], g2r.at[q, x], xo[n], z)
                )

    def lead_y():
        for first_slot, count in ((0, 4), (4, 2)):
            q = first_slot // 4
            for d in (1, 3, 2):
                xx = lax.rem(x + d, 4)
                part = lead.at[h, pl.ds(first_slot, count), rows(y, xx)]
                pl.when((h == 1) | (q == 0))(copy(part, part, g2s.at[q, 0], g2r.at[q, xx], sib, z).wait_recv)
            part = lead.at[h, pl.ds(first_slot, count), pl.ds(pl.multiple_of(32 * y, 32), 32)]
            for n in range(3):
                send((h == 1) | (q == 0), copy(part, part, g3s.at[q, n], g3r.at[q, y], yo[n], z))

    def lead_s():
        for first_slot, count in ((0, 4), (4, 2)):
            q = first_slot // 4
            for d in (1, 3, 2):
                yy = lax.rem(y + d, 4)
                part = lead.at[h, pl.ds(first_slot, count), pl.ds(pl.multiple_of(32 * yy, 32), 32)]
                pl.when((h == 1) | (q == 0))(copy(part, part, g3s.at[q, 0], g3r.at[q, yy], sib, z).wait_recv)
            part = lead.at[h, pl.ds(first_slot, count)]
            send((h == 1) | (q == 0), copy(part, part, g4s.at[q], g4r.at[q], sib, z))

    def lead_arrived(i):
        if i == 0:
            pl.when(h == 1)(copy(first, first, f4s, fr, sib, z).wait_recv)
        if i == 1:
            part = lead.at[1 - h, pl.ds(0, 4)]
            copy(part, part, g4s.at[0], g4r.at[0], sib, z).wait_recv()
            part = lead.at[1 - h, pl.ds(4, 2)]
            pl.when(h == 0)(copy(part, part, g4s.at[1], g4r.at[1], sib, z).wait_recv)

    steps = factor_lead(lead, m2, s, inverse, diag, lead_arrived)

    def work(count):
        for _ in range(count):
            next(steps, None)

    first_z()
    lead_scatter()
    z_event(0)
    lead_planes()
    z_event(1)
    first_y()
    x_event(0)
    z_event(2)
    first_x()
    lead_x()
    x_event(1)
    for n in range(3):
        y_event(0, n)
    z_event(3)
    first_s()
    lead_y()
    work(4)
    x_event(2)
    for n in range(3):
        work(4)
        y_event(1, n)
    lead_s()
    z_event(4)
    work(4)
    x_event(3)
    for n in range(3):
        work(4)
        y_event(2, n)
    z_event(5)
    work(4)
    x_event(4)
    for n in range(3):
        work(4)
        y_event(3, n)
    work(4)
    x_event(5)
    for n in range(3):
        work(4)
        y_event(4, n)
    for n in range(3):
        work(4)
        y_event(5, n)
    for _ in steps:
        pass

    for yy in range(4):
        for k in range(4):
            block = right.at[yy, k, other]
            copy(block, block, ss.at[yy, k], sr.at[yy, k], sib, z).wait_recv()
    for cond, desc in sends:
        pl.when(cond)(desc.wait_send)


def exchange(ids, coupled, values):
    dma = pltpu.SemaphoreType.DMA
    vmem = pl.BlockSpec(memory_space=pltpu.VMEM)
    return pl.pallas_call(
        exchange_kernel,
        out_shape=(
            jax.ShapeDtypeStruct((4, 4, B, B), F32),
            jax.ShapeDtypeStruct((4, 4, 4, B, B), F32),
            jax.ShapeDtypeStruct((512, 512), F32),
            jax.ShapeDtypeStruct((4, B, B), F32),
        ),
        in_specs=[
            pl.BlockSpec(memory_space=pltpu.SMEM),
            pl.BlockSpec(memory_space=pltpu.SMEM),
            pl.BlockSpec(memory_space=pltpu.HBM),
        ],
        out_specs=(vmem, vmem, vmem, vmem),
        scratch_shapes=[
            pltpu.VMEM((SLOTS, B, B), F32),
            pltpu.VMEM((2, 6, B, B), F32),
            pltpu.VMEM((B, 2 * B), F32),
            pltpu.VMEM((512, 512), F32),
            dma,
            dma((4, 4)), dma((4, 4)), dma((4, 4)),
            dma((4, 3)), dma((4,)), dma((4,)),
            dma((4, 2)), dma((4, 4)), dma((4, 2)), dma((4, 2)),
            dma((4, 4)), dma((4, 4)),
            dma, dma((7,)), dma((3,)), dma((3,)), dma,
            dma((15,)), dma((2,)),
            dma((2, 7)), dma((2, 4)),
            dma((2, 3)), dma((2, 4)),
            dma((2, 3)), dma((2, 4)),
            dma((2,)), dma((2,)),
        ],
        compiler_params=pltpu.CompilerParams(
            collective_id=0, has_side_effects=True, vmem_limit_bytes=46 << 20
        ),
        name="exchange",
    )(ids, coupled, values)


def eliminate(m2):
    sub = lax.broadcasted_iota(jnp.int32, (8, B), 0)
    nt = NB // 8
    for p in range(B // NB):
        b = NB * p
        for u in range(nt):
            cb = b + 8 * u
            T = {
                (i, t): m2[b + 8 * i : b + 8 * i + 8, B * t : B * t + B] for t in range(2) for i in range(u, nt)
            }
            C = {
                (i, j): jnp.broadcast_to(T[i, 0][:, cb + j : cb + j + 1], (8, B))
                for i in range(u, nt)
                for j in range(8)
            }
            sc = jnp.ones((8, B), F32)
            for j in range(8):
                piv = jnp.broadcast_to(C[u, j][j : j + 1, :], (8, B))
                inv = 1.0 / piv
                sc = jnp.where(sub == j, lax.rsqrt(piv), sc)
                rows = [jnp.broadcast_to(T[u, t][j : j + 1, :], (8, B)) for t in range(2)]
                cs = {jj: jnp.broadcast_to(C[u, jj][j : j + 1, :], (8, B)) for jj in range(j + 1, 8)}
                for i in range(u, nt):
                    m = C[i, j] * inv
                    if i == u:
                        if j == 7:
                            continue
                        m = jnp.where(sub > j, m, 0.0)
                    for jj in range(j + 1, 8):
                        C[i, jj] = C[i, jj] - m * cs[jj]
                    for t in range(2):
                        T[i, t] = T[i, t] - m * rows[t]
            for t in range(2):
                T[u, t] = T[u, t] * sc
            for (i, t), v in T.items():
                m2[b + 8 * i : b + 8 * i + 8, B * t : B * t + B] = v
            yield
        if b + NB < B:
            R = m2[b : b + NB, :]
            g = lax.dot_general(
                R[:, b + NB : B], R, (((0,), (0,)), ((), ())), precision=HIGH, preferred_element_type=F32
            )
            m2[b + NB : B, :] = m2[b + NB : B, :] - g
            yield


def factor_lead(lead, m2, s, e, diag, arrived):
    n = 4
    ri = lax.broadcasted_iota(jnp.int32, (B, B), 0)
    ci = lax.broadcasted_iota(jnp.int32, (B, B), 1)
    e[...] = jnp.zeros_like(e)
    for k in range(n):
        a, z = B * k, B * k + B
        if k == 0:
            arrived(0)
            m2[:, :B] = lead[0, 4]
        else:
            m2[:, :B] = s[a:z, a:z]
        m2[:, B:] = jnp.where(ri == ci, 1.0, 0.0).astype(F32)
        yield from eliminate(m2)
        if k == 0:
            for i in range(1, n):
                arrived(i)
                base = 4 if i < 2 else 0
                s[B * i : B * i + B, B * i : B * i + B] = lead[i % 2, base + i]
                for kk in range(i):
                    s[B * kk : B * kk + B, B * i : B * i + B] = lead[i % 2, base + kk].T
            yield
        li = jnp.where(ri >= ci, m2[:, B:], 0.0)
        diag[k] = jnp.where(ri >= ci, m2[:, :B].T, 0.0)
        parts = []
        if k < n - 1:
            parts.append(s[a:z, z:])
        if k > 0:
            parts.append(e[a:z, :a])
        R = jnp.dot(li, jnp.concatenate(parts, axis=1), precision=HIGH, preferred_element_type=F32)
        w = (n - 1 - k) * B
        if k > 0:
            e[a:z, :a] = R[:, w:]
        e[a:z, a:z] = li
        if k < n - 1:
            s[a:z, z:] = R[:, :w]
            yield
            full = jnp.concatenate([s[a:z, z:], e[a:z, :z]], axis=1)
            g = lax.dot_general(
                full[:, :w], full, (((0,), (0,)), ((), ())), precision=HIGH, preferred_element_type=F32
            )
            s[z:, z:] = s[z:, z:] - g[:, :w]
            e[z:, :z] = e[z:, :z] - g[:, w:]
        yield


def split(v):
    hi = v.astype(BF16)
    return hi, (v - hi.astype(F32)).astype(BF16)


def dot_nt(a, b):
    (ah, al), (bh, bl) = a, b
    return lax.dot_general(
        jnp.concatenate([ah, al, ah], axis=1),
        jnp.concatenate([bh, bh, bl], axis=1),
        (((1,), (1,)), ((), ())),
        preferred_element_type=F32,
    )


def finish_kernel(
    ids, coupled, values, left, right, inverse, diag, out,
    obuf, ehi, elo, whi, wlo, g, osem,
):
    r = lax.axis_index("row")
    hi, lo = split(inverse[...])
    ehi[...] = hi
    elo[...] = lo

    def factor_rows(blocks):
        cat = [blocks[k].reshape(4 * B, B) for k in range(4)]
        parts = [split(c) for c in cat]
        xh = jnp.concatenate([p[0] for p in parts], axis=1)
        xl = jnp.concatenate([p[1] for p in parts], axis=1)
        h = 2 * B
        w0 = dot_nt((xh[:, :h], xl[:, :h]), (ehi[:h, :h], elo[:h, :h]))
        w1 = dot_nt((xh, xl), (ehi[h:, :], elo[h:, :]))
        return jnp.concatenate([w0, w1], axis=1)

    wl = factor_rows(left)
    for n in range(4):
        for a in range(4):
            g[64 + 4 * n + a] = -wl[B * a : B * a + B, B * n : B * n + B]
    g[80] = jnp.zeros((B, B), F32)

    @pl.when(r < 4)
    def _():
        g[64 + 4 * r] = -diag[r]

    hi, lo = split(wl)
    whi[...] = hi
    wlo[...] = lo

    @pl.loop(0, 4)
    def _(y):
        wr = factor_rows(right.at[y])
        wrh, wrl = split(wr)
        for c in range(2):
            p = dot_nt((whi[...], wlo[...]), (wrh[256 * c : 256 * c + 256], wrl[256 * c : 256 * c + 256]))
            for b in range(2):
                for a in range(4):
                    g[(y * 4 + 2 * c + b) * 4 + a] = p[B * a : B * a + B, B * b : B * b + B]

    @pl.loop(0, SLOTS, unroll=4)
    def _(slot):
        i = ids[0, slot]
        j = ids[1, slot]
        a = jnp.int32(0)
        own = jnp.int32(0)
        b = jnp.int32(0)
        r2 = j & 31
        for n in range(4):
            hit = i == coupled[n, r]
            a = jnp.where(hit, n, a)
            own = jnp.where(hit, 1, own)
            b = jnp.where(j == coupled[n, r2], n, b)
        found = own == 1
        trailing = found & (j >= 4)
        panel = found & (j < 4)
        place = jnp.where(trailing, ((r2 // 8) * 4 + b) * 4 + a, jnp.where(panel, 64 + 4 * j + a, 80))
        keep = (i >= 0) & jnp.logical_not(panel)
        obuf[slot] = jnp.where(keep, values[slot], 0.0) - g[place]
        pltpu.make_async_copy(obuf.at[slot], out.at[slot], osem).start()

    pltpu.make_async_copy(obuf, out, osem).wait()


def finish(ids, coupled, values, left, right, inverse, diag):
    smem = pl.BlockSpec(memory_space=pltpu.SMEM)
    vmem = pl.BlockSpec(memory_space=pltpu.VMEM)
    hbm = pl.BlockSpec(memory_space=pltpu.HBM)
    dma = pltpu.SemaphoreType.DMA
    return pl.pallas_call(
        finish_kernel,
        out_shape=jax.ShapeDtypeStruct((SLOTS, B, B), F32),
        in_specs=[smem, smem, vmem, vmem, vmem, vmem, vmem],
        out_specs=hbm,
        scratch_shapes=[
            pltpu.VMEM((SLOTS, B, B), F32),
            pltpu.VMEM((512, 512), BF16),
            pltpu.VMEM((512, 512), BF16),
            pltpu.VMEM((512, 512), BF16),
            pltpu.VMEM((512, 512), BF16),
            pltpu.VMEM((81, B, B), F32),
            dma,
        ],
        compiler_params=pltpu.CompilerParams(vmem_limit_bytes=32 << 20),
        name="finish",
    )(ids, coupled, values, left, right, inverse, diag)


def body(values, block_ids, coupled_rows):
    ids = block_ids[0, 0].T
    coupled = coupled_rows.T
    left, right, inverse, diag = exchange(ids, coupled, values[0, 0])
    out = finish(ids, coupled, values[0, 0], left, right, inverse, diag)
    return out[None, None]


def solution(mesh):
    placed = (P("row", "col", None, None, None), P("row", "col", None, None), P())
    return jax.shard_map(
        body,
        mesh=mesh,
        in_specs=placed,
        out_specs=P("row", "col", None, None, None),
        check_vma=False,
    )
```

```python
import jax
import jax.numpy as jnp
from jax import lax
from jax.experimental import pallas as pl
from jax.experimental.pallas import tpu as pltpu
from jax.sharding import PartitionSpec as P

B = 128
NB = 32
SLOTS = 68
HIGH = lax.Precision.HIGHEST
MESH = pl.DeviceIdType.MESH
F32 = jnp.float32
BF16 = jnp.bfloat16


def exchange_kernel(
    ids, coupled, values, left, right, inverse, diag, vbuf, lead, m2, s, vsem,
    zus, zds, zr, xs, xr, os_, ys, yr, yfs, yfr, ss, sr, fr, f1s, f2s, f3s, f4s,
    g0s, g0r, g1s, g1r, g2s, g2r, g3s, g3r, g4s, g4r,
):
    r = lax.axis_index("row")
    z = lax.axis_index("col")
    h = lax.rem(r, 2)
    x = lax.rem(r // 2, 4)
    y = r // 8
    up = lax.rem(z + 1, 8)
    down = lax.rem(z + 7, 8)
    sib = r + 1 - 2 * h
    xo = [y * 8 + lax.rem(x + d, 4) * 2 + h for d in (1, 3, 2)]
    yo = [lax.rem(y + d, 4) * 8 + x * 2 + h for d in (1, 3, 2)]
    origin = x == z // 2
    source = origin & (h == lax.rem(z, 2))
    true = r >= 0

    load = pltpu.make_async_copy(values, vbuf, vsem)
    pl.when(z < 4)(load.start)

    barrier = pltpu.get_barrier_semaphore()

    def greet(row, col):
        pl.semaphore_signal(barrier, inc=1, device_id={"row": row, "col": col}, device_id_type=MESH)

    for d in range(1, 8):
        greet(r, lax.rem(z + d, 8))
    for d in range(1, 16):
        greet(lax.rem(r + 2 * d, 32), z)
    greet(sib, z)

    def scan(slot, found):
        i = ids[0, slot]
        hit = ids[1, slot] == z
        return tuple(jnp.where(hit & (i == coupled[a, r]), slot, found[a]) for a in range(4))

    found = lax.fori_loop(0, SLOTS, scan, (jnp.int32(-1),) * 4)
    pl.semaphore_wait(barrier, 23)

    @pl.when(z < 4)
    def _():
        load.wait()
        for a in range(4):
            block = vbuf[jnp.maximum(found[a], 0)]
            left[z, a] = jnp.where(found[a] >= 0, block, 0.0)

    def copy(src, dst, ssem, rsem, row, col):
        return pltpu.make_async_remote_copy(
            src_ref=src, dst_ref=dst, send_sem=ssem, recv_sem=rsem,
            device_id={"row": row, "col": col}, device_id_type=MESH,
        )

    sends = []

    def send(cond, *descs):
        @pl.when(cond)
        def _():
            for desc in descs:
                desc.start()

        sends.append((cond, descs))

    def post(cond, arrived, descs):
        @pl.when(cond)
        def _():
            for desc in arrived:
                desc.wait_recv()
            for desc in descs:
                desc.start()


    def travellers(d):
        if d == 0:
            return [(jnp.minimum(z, 3), z < 4, true, true)]
        ku = lax.rem(z + 8 - d, 8)
        reach = jnp.where(ku >= 2, 5, 2)
        kd = lax.rem(z + d, 8)
        depth = jnp.where(kd >= 2, 2, 5)
        return [
            (jnp.minimum(ku, 3), (ku <= 3) & (d <= reach), d < reach, None),
            (jnp.minimum(kd, 3), (kd <= 3) & (d <= depth), None, d < depth),
        ]

    def spread(k, q):
        block = right.at[y, k, 2 * h + q]
        return [copy(block, block, ys.at[k, n, q], yr.at[y, k, q], yo[n], z) for n in range(2)] + [
            copy(block, block, ss.at[y, k, q], sr.at[y, k, q], sib, z)
        ]

    def spread_x(k, q):
        block = right.at[y, k, 2 * h + q]
        return [copy(block, block, xs.at[k, n, q], xr.at[k, q], xo[n], z) for n in range(3)]

    def to_sibling(k, q):
        a = 2 - 2 * h + q
        return copy(left.at[k, a], right.at[y, k, a], os_.at[k, q], xr.at[k, q], sib, z)

    def z_event(d):
        group = travellers(d)
        for a in range(4):
            for k, valid, go_up, go_down in group:
                block = left.at[k, a]
                rise = copy(block, block, zus.at[k, a], zr.at[k, a], r, up)
                sink = copy(block, block, zds.at[k, a], zr.at[k, a], r, down)
                if d == 0:
                    post(valid, [], [rise, sink])
                elif go_up is not None:
                    post(valid, [rise], [])
                    post(valid & go_up, [], [rise])
                else:
                    post(valid, [sink], [])
                    post(valid & go_down, [], [sink])
                q = a % 2
                post(valid & source & (h != a // 2), [], [to_sibling(k, q)])

                @pl.when(valid & source & (h == a // 2))
                def _():
                    right[y, k, a] = left[k, a]
                    for desc in spread_x(k, q) + spread(k, q):
                        desc.start()

    def x_event(d):
        for k, valid, _, _ in travellers(d):
            mine = valid & jnp.logical_not(source)
            for q in range(2):
                block = right.at[y, k, 2 * h + q]
                post(mine, [copy(block, block, os_.at[k, q], xr.at[k, q], sib, z)], [])
                post(mine & origin, [], spread_x(k, q))
                post(mine, [], spread(k, q))

    def y_event(d, n):
        yy = lax.rem(y + (1, 3, 2)[n], 4)
        for k, valid, _, _ in travellers(d):
            part = lambda q: right.at[yy, k, 2 * h + q]
            on = lambda q, to: copy(part(q), part(q), yfs.at[k, q], yfr.at[k, q], to, z)
            share = lambda q: copy(part(q), part(q), ss.at[yy, k, q], sr.at[yy, k, q], sib, z)
            for q in (1 - n, n) if n < 2 else (0, 1):
                if n == 2:
                    post(valid, [on(q, yo[q])], [share(q)])
                else:
                    come = copy(part(q), part(q), ys.at[k, n, q], yr.at[yy, k, q], yo[n], z)
                    post(valid, [come], ([on(q, yo[1 - n])] if q == 1 - n else []) + [share(q)])

    first = lead.at[0, 4]

    def first_z():
        mine = (r == 0) & (z == 0)

        @pl.when(mine)
        def _():
            lead[0, 4] = left[0, 0]

        send(mine, *[copy(first, first, f1s.at[d - 1], fr, r, lax.rem(z + d, 8)) for d in range(1, 8)])

    def first_out(mine):
        send(
            mine,
            *[copy(first, first, f3s.at[n], fr, xo[n], z) for n in range(3)],
            copy(first, first, f4s, fr, sib, z),
        )

    def first_y():
        mine = r == 0
        pl.when(mine & (z != 0))(copy(first, first, f4s, fr, sib, z).wait_recv)
        send(mine, *[copy(first, first, f2s.at[n], fr, yo[n], z) for n in range(3)])
        first_out(mine)

    def first_x():
        mine = (h == 0) & (x == 0) & (y > 0)
        pl.when(mine)(copy(first, first, f4s, fr, sib, z).wait_recv)
        first_out(mine)

    def first_s():
        mine = (h == 0) & (x > 0)
        pl.when(mine)(copy(first, first, f4s, fr, sib, z).wait_recv)
        send(mine, copy(first, first, f4s, fr, sib, z))

    rows = lambda yy, xx: pl.ds(pl.multiple_of(32 * yy + 8 * xx, 8), 8)
    mine8 = rows(y, x)
    zc = jnp.minimum(z, 3)

    def here(j, k):
        i = 2 * j + h
        return (i >= k) & (i > 0)

    def slot_of(j, k):
        return k if j else 4 + jnp.minimum(k, 1)

    def lead_scatter():
        for j in range(2):
            mine = (r == 2 * j + h) & (z < 4) & here(j, z)
            slot = slot_of(j, zc)

            @pl.when(mine)
            def _():
                lead[h, slot, mine8] = left[zc, 0, mine8]

            descs = []
            for d in range(1, 16):
                p = lax.rem(y * 4 + x + d, 16)
                at = rows(p // 4, lax.rem(p, 4))
                part, target = left.at[zc, 0, at], lead.at[h, slot, at]
                descs.append(copy(part, target, g0s.at[d - 1], g0r.at[j], p * 2 + h, z))
            send(mine, *descs)

    def lead_planes():
        @pl.when(h == 0)
        def _():
            lead[0, 5, mine8] = jnp.zeros((8, B), F32)
            lead[0, 3, mine8] = jnp.zeros((8, B), F32)

        for j in range(2):
            mine = (z < 4) & here(j, z)
            part = lead.at[h, slot_of(j, zc), mine8]
            pl.when(mine & (r != 2 * j + h))(copy(part, part, g0s.at[0], g0r.at[j], sib, z).wait_recv)
            send(
                mine,
                *[
                    copy(part, part, g1s.at[j, d - 1], g1r.at[j, zc], r, lax.rem(z + d, 8))
                    for d in range(1, 8)
                ],
            )

    def lead_x():
        for j in range(2):
            for k in range(4 if j else 2):
                part = lead.at[h, slot_of(j, k), mine8]
                pl.when(here(j, k) & (z != k))(copy(part, part, g1s.at[j, 0], g1r.at[j, k], r, up).wait_recv)
        for first_slot, count in ((0, 4), (4, 2)):
            q = first_slot // 4
            part = lead.at[h, pl.ds(first_slot, count), mine8]
            send(
                (h == 1) | (q == 0),
                *[copy(part, part, g2s.at[q, n], g2r.at[q, x], xo[n], z) for n in range(3)],
            )

    def lead_y():
        for first_slot, count in ((0, 4), (4, 2)):
            q = first_slot // 4
            for d in (1, 3, 2):
                xx = lax.rem(x + d, 4)
                part = lead.at[h, pl.ds(first_slot, count), rows(y, xx)]
                pl.when((h == 1) | (q == 0))(copy(part, part, g2s.at[q, 0], g2r.at[q, xx], sib, z).wait_recv)
            part = lead.at[h, pl.ds(first_slot, count), pl.ds(pl.multiple_of(32 * y, 32), 32)]
            send(
                (h == 1) | (q == 0),
                *[copy(part, part, g3s.at[q, n], g3r.at[q, y], yo[n], z) for n in range(3)],
            )

    def lead_s():
        for first_slot, count in ((0, 4), (4, 2)):
            q = first_slot // 4
            for d in (1, 3, 2):
                yy = lax.rem(y + d, 4)
                part = lead.at[h, pl.ds(first_slot, count), pl.ds(pl.multiple_of(32 * yy, 32), 32)]
                pl.when((h == 1) | (q == 0))(copy(part, part, g3s.at[q, 0], g3r.at[q, yy], sib, z).wait_recv)
            part = lead.at[h, pl.ds(first_slot, count)]
            send((h == 1) | (q == 0), copy(part, part, g4s.at[q], g4r.at[q], sib, z))

    def lead_arrived(i):
        if i == 0:
            pl.when(h == 1)(copy(first, first, f4s, fr, sib, z).wait_recv)
        if i == 1:
            part = lead.at[1 - h, pl.ds(0, 4)]
            copy(part, part, g4s.at[0], g4r.at[0], sib, z).wait_recv()
            part = lead.at[1 - h, pl.ds(4, 2)]
            pl.when(h == 0)(copy(part, part, g4s.at[1], g4r.at[1], sib, z).wait_recv)

    steps = factor_lead(lead, m2, s, inverse, diag, lead_arrived)

    def work(count):
        for _ in range(count):
            next(steps, None)

    first_z()
    lead_scatter()
    z_event(0)
    lead_planes()
    z_event(1)
    first_y()
    x_event(0)
    z_event(2)
    first_x()
    lead_x()
    x_event(1)
    for n in range(3):
        y_event(0, n)
    z_event(3)
    first_s()
    lead_y()
    work(4)
    x_event(2)
    for n in range(3):
        work(4)
        y_event(1, n)
    lead_s()
    z_event(4)
    work(6)
    x_event(3)
    for n in range(3):
        work(6)
        y_event(2, n)
    z_event(5)
    work(6)
    x_event(4)
    for n in range(3):
        work(6)
        y_event(3, n)
    work(6)
    x_event(5)
    for n in range(3):
        work(6)
        y_event(4, n)
    for n in range(3):
        work(6)
        y_event(5, n)
    for _ in steps:
        pass

    for yy in range(4):
        for k in range(4):
            for q in range(2):
                block = right.at[yy, k, 2 - 2 * h + q]
                copy(block, block, ss.at[yy, k, q], sr.at[yy, k, q], sib, z).wait_recv()
    for cond, descs in sends:

        @pl.when(cond)
        def _():
            for desc in descs:
                desc.wait_send()

    for k in range(4):

        @pl.when(lax.rem(z + 8 - k, 8) < (5 if k >= 2 else 2))
        def _():
            for a in range(4):
                block = left.at[k, a]
                copy(block, block, zus.at[k, a], zr.at[k, a], r, up).wait_send()

        @pl.when(lax.rem(k + 8 - z, 8) < (2 if k >= 2 else 5))
        def _():
            for a in range(4):
                block = left.at[k, a]
                copy(block, block, zds.at[k, a], zr.at[k, a], r, down).wait_send()

        for q in range(2):
            pl.when(source)(to_sibling(k, q).wait_send)

            @pl.when(origin)
            def _():
                for desc in spread_x(k, q):
                    desc.wait_send()

            for desc in spread(k, q):
                desc.wait_send()
            part = right.at[y, k, q]
            copy(part, part, yfs.at[k, q], yfr.at[k, q], yo[q], z).wait_send()
            for n in range(3):
                yy = lax.rem(y + (1, 3, 2)[n], 4)
                block = right.at[yy, k, 2 * h + q]
                copy(block, block, ss.at[yy, k, q], sr.at[yy, k, q], sib, z).wait_send()


def exchange(ids, coupled, values):
    dma = pltpu.SemaphoreType.DMA
    vmem = pl.BlockSpec(memory_space=pltpu.VMEM)
    return pl.pallas_call(
        exchange_kernel,
        out_shape=(
            jax.ShapeDtypeStruct((4, 4, B, B), F32),
            jax.ShapeDtypeStruct((4, 4, 4, B, B), F32),
            jax.ShapeDtypeStruct((512, 512), F32),
            jax.ShapeDtypeStruct((4, B, B), F32),
        ),
        in_specs=[
            pl.BlockSpec(memory_space=pltpu.SMEM),
            pl.BlockSpec(memory_space=pltpu.SMEM),
            pl.BlockSpec(memory_space=pltpu.HBM),
        ],
        out_specs=(vmem, vmem, vmem, vmem),
        scratch_shapes=[
            pltpu.VMEM((SLOTS, B, B), F32),
            pltpu.VMEM((2, 6, B, B), F32),
            pltpu.VMEM((B, 2 * B), F32),
            pltpu.VMEM((512, 512), F32),
            dma,
            dma((4, 4)), dma((4, 4)), dma((4, 4)),
            dma((4, 3, 2)), dma((4, 2)), dma((4, 2)),
            dma((4, 2, 2)), dma((4, 4, 2)), dma((4, 2)), dma((4, 2)),
            dma((4, 4, 2)), dma((4, 4, 2)),
            dma, dma((7,)), dma((3,)), dma((3,)), dma,
            dma((15,)), dma((2,)),
            dma((2, 7)), dma((2, 4)),
            dma((2, 3)), dma((2, 4)),
            dma((2, 3)), dma((2, 4)),
            dma((2,)), dma((2,)),
        ],
        compiler_params=pltpu.CompilerParams(
            collective_id=0, has_side_effects=True, vmem_limit_bytes=46 << 20
        ),
        name="exchange",
    )(ids, coupled, values)


def eliminate(m2):
    sub = lax.broadcasted_iota(jnp.int32, (8, B), 0)
    nt = NB // 8
    for p in range(B // NB):
        b = NB * p
        for u in range(nt):
            cb = b + 8 * u
            T = {
                (i, t): m2[b + 8 * i : b + 8 * i + 8, B * t : B * t + B] for t in range(2) for i in range(u, nt)
            }
            C = {
                (i, j): jnp.broadcast_to(T[i, 0][:, cb + j : cb + j + 1], (8, B))
                for i in range(u, nt)
                for j in range(8)
            }
            sc = jnp.ones((8, B), F32)
            for j in range(8):
                piv = jnp.broadcast_to(C[u, j][j : j + 1, :], (8, B))
                inv = 1.0 / piv
                sc = jnp.where(sub == j, lax.rsqrt(piv), sc)
                rows = [jnp.broadcast_to(T[u, t][j : j + 1, :], (8, B)) for t in range(2)]
                cs = {jj: jnp.broadcast_to(C[u, jj][j : j + 1, :], (8, B)) for jj in range(j + 1, 8)}
                for i in range(u, nt):
                    m = C[i, j] * inv
                    if i == u:
                        if j == 7:
                            continue
                        m = jnp.where(sub > j, m, 0.0)
                    for jj in range(j + 1, 8):
                        C[i, jj] = C[i, jj] - m * cs[jj]
                    for t in range(2):
                        T[i, t] = T[i, t] - m * rows[t]
            for t in range(2):
                T[u, t] = T[u, t] * sc
            for (i, t), v in T.items():
                m2[b + 8 * i : b + 8 * i + 8, B * t : B * t + B] = v
            yield
        if b + NB < B:
            R = m2[b : b + NB, :]
            g = lax.dot_general(
                R[:, b + NB : B], R, (((0,), (0,)), ((), ())), precision=HIGH, preferred_element_type=F32
            )
            m2[b + NB : B, :] = m2[b + NB : B, :] - g
            yield


def factor_lead(lead, m2, s, e, diag, arrived):
    n = 4
    ri = lax.broadcasted_iota(jnp.int32, (B, B), 0)
    ci = lax.broadcasted_iota(jnp.int32, (B, B), 1)
    e[...] = jnp.zeros_like(e)
    for k in range(n):
        a, z = B * k, B * k + B
        if k == 0:
            arrived(0)
            m2[:, :B] = lead[0, 4]
        else:
            m2[:, :B] = s[a:z, a:z]
        m2[:, B:] = jnp.where(ri == ci, 1.0, 0.0).astype(F32)
        yield from eliminate(m2)
        if k == 0:
            for i in range(1, n):
                arrived(i)
                base = 4 if i < 2 else 0
                s[B * i : B * i + B, B * i : B * i + B] = lead[i % 2, base + i]
                for kk in range(i):
                    s[B * kk : B * kk + B, B * i : B * i + B] = lead[i % 2, base + kk].T
            yield
        li = jnp.where(ri >= ci, m2[:, B:], 0.0)
        diag[k] = jnp.where(ri >= ci, m2[:, :B].T, 0.0)
        parts = []
        if k < n - 1:
            parts.append(s[a:z, z:])
        if k > 0:
            parts.append(e[a:z, :a])
        R = jnp.dot(li, jnp.concatenate(parts, axis=1), precision=HIGH, preferred_element_type=F32)
        w = (n - 1 - k) * B
        if k > 0:
            e[a:z, :a] = R[:, w:]
        e[a:z, a:z] = li
        if k < n - 1:
            s[a:z, z:] = R[:, :w]
            yield
            full = jnp.concatenate([s[a:z, z:], e[a:z, :z]], axis=1)
            g = lax.dot_general(
                full[:, :w], full, (((0,), (0,)), ((), ())), precision=HIGH, preferred_element_type=F32
            )
            s[z:, z:] = s[z:, z:] - g[:, :w]
            e[z:, :z] = e[z:, :z] - g[:, w:]
        yield


def split(v):
    hi = v.astype(BF16)
    return hi, (v - hi.astype(F32)).astype(BF16)


def dot_nt(a, b):
    (ah, al), (bh, bl) = a, b
    return lax.dot_general(
        jnp.concatenate([ah, al, ah], axis=1),
        jnp.concatenate([bh, bh, bl], axis=1),
        (((1,), (1,)), ((), ())),
        preferred_element_type=F32,
    )


def finish_kernel(
    ids, coupled, values, left, right, inverse, diag, out,
    obuf, ehi, elo, whi, wlo, g, osem,
):
    r = lax.axis_index("row")
    hi, lo = split(inverse[...])
    ehi[...] = hi
    elo[...] = lo

    def factor_rows(blocks):
        cat = [blocks[k].reshape(4 * B, B) for k in range(4)]
        parts = [split(c) for c in cat]
        xh = jnp.concatenate([p[0] for p in parts], axis=1)
        xl = jnp.concatenate([p[1] for p in parts], axis=1)
        h = 2 * B
        w0 = dot_nt((xh[:, :h], xl[:, :h]), (ehi[:h, :h], elo[:h, :h]))
        w1 = dot_nt((xh, xl), (ehi[h:, :], elo[h:, :]))
        return jnp.concatenate([w0, w1], axis=1)

    wl = factor_rows(left)
    for n in range(4):
        for a in range(4):
            g[64 + 4 * n + a] = -wl[B * a : B * a + B, B * n : B * n + B]
    g[80] = jnp.zeros((B, B), F32)

    @pl.when(r < 4)
    def _():
        g[64 + 4 * r] = -diag[r]

    hi, lo = split(wl)
    whi[...] = hi
    wlo[...] = lo

    @pl.loop(0, 4)
    def _(y):
        wr = factor_rows(right.at[y])
        wrh, wrl = split(wr)
        for c in range(2):
            p = dot_nt((whi[...], wlo[...]), (wrh[256 * c : 256 * c + 256], wrl[256 * c : 256 * c + 256]))
            for b in range(2):
                for a in range(4):
                    g[(y * 4 + 2 * c + b) * 4 + a] = p[B * a : B * a + B, B * b : B * b + B]

    @pl.loop(0, SLOTS, unroll=4)
    def _(slot):
        i = ids[0, slot]
        j = ids[1, slot]
        a = jnp.int32(0)
        own = jnp.int32(0)
        b = jnp.int32(0)
        r2 = j & 31
        for n in range(4):
            hit = i == coupled[n, r]
            a = jnp.where(hit, n, a)
            own = jnp.where(hit, 1, own)
            b = jnp.where(j == coupled[n, r2], n, b)
        found = own == 1
        trailing = found & (j >= 4)
        panel = found & (j < 4)
        place = jnp.where(trailing, ((r2 // 8) * 4 + b) * 4 + a, jnp.where(panel, 64 + 4 * j + a, 80))
        keep = (i >= 0) & jnp.logical_not(panel)
        obuf[slot] = jnp.where(keep, values[slot], 0.0) - g[place]
        pltpu.make_async_copy(obuf.at[slot], out.at[slot], osem).start()

    pltpu.make_async_copy(obuf, out, osem).wait()


def finish(ids, coupled, values, left, right, inverse, diag):
    smem = pl.BlockSpec(memory_space=pltpu.SMEM)
    vmem = pl.BlockSpec(memory_space=pltpu.VMEM)
    hbm = pl.BlockSpec(memory_space=pltpu.HBM)
    dma = pltpu.SemaphoreType.DMA
    return pl.pallas_call(
        finish_kernel,
        out_shape=jax.ShapeDtypeStruct((SLOTS, B, B), F32),
        in_specs=[smem, smem, vmem, vmem, vmem, vmem, vmem],
        out_specs=hbm,
        scratch_shapes=[
            pltpu.VMEM((SLOTS, B, B), F32),
            pltpu.VMEM((512, 512), BF16),
            pltpu.VMEM((512, 512), BF16),
            pltpu.VMEM((512, 512), BF16),
            pltpu.VMEM((512, 512), BF16),
            pltpu.VMEM((81, B, B), F32),
            dma,
        ],
        compiler_params=pltpu.CompilerParams(vmem_limit_bytes=32 << 20),
        name="finish",
    )(ids, coupled, values, left, right, inverse, diag)


def body(values, block_ids, coupled_rows):
    ids = block_ids[0, 0].T
    coupled = coupled_rows.T
    left, right, inverse, diag = exchange(ids, coupled, values[0, 0])
    out = finish(ids, coupled, values[0, 0], left, right, inverse, diag)
    return out[None, None]


def solution(mesh):
    placed = (P("row", "col", None, None, None), P("row", "col", None, None), P())
    return jax.shard_map(
        body,
        mesh=mesh,
        in_specs=placed,
        out_specs=P("row", "col", None, None, None),
        check_vma=False,
    )
```

```python
import jax
import jax.numpy as jnp
from jax import lax
from jax.experimental import pallas as pl
from jax.experimental.pallas import tpu as pltpu
from jax.sharding import PartitionSpec as P

B = 128
NB = 32
SLOTS = 68
HIGH = lax.Precision.HIGHEST
MESH = pl.DeviceIdType.MESH
F32 = jnp.float32
BF16 = jnp.bfloat16


def exchange_kernel(
    ids, coupled, values, left, right, inverse, diag, vbuf, lead, m2, s, vsem,
    zus, zds, zr, xs, xr, os_, ys, yr, yfs, yfr, ss, sr, fr, f1s, f2s, f3s, f4s,
    g0s, g0r, g1s, g1r, g2s, g2r, g3s, g3r, g4s, g4r,
):
    r = lax.axis_index("row")
    z = lax.axis_index("col")
    h = lax.rem(r, 2)
    x = lax.rem(r // 2, 4)
    y = r // 8
    up = lax.rem(z + 1, 8)
    down = lax.rem(z + 7, 8)
    sib = r + 1 - 2 * h
    xo = [y * 8 + lax.rem(x + d, 4) * 2 + h for d in (1, 3, 2)]
    yo = [lax.rem(y + d, 4) * 8 + x * 2 + h for d in (1, 3, 2)]
    origin = x == z // 2
    source = origin & (h == lax.rem(z, 2))
    true = r >= 0

    load = pltpu.make_async_copy(values, vbuf, vsem)
    pl.when(z < 4)(load.start)

    barrier = pltpu.get_barrier_semaphore()

    def greet(row, col):
        pl.semaphore_signal(barrier, inc=1, device_id={"row": row, "col": col}, device_id_type=MESH)

    for d in range(1, 8):
        greet(r, lax.rem(z + d, 8))
    for d in range(1, 16):
        greet(lax.rem(r + 2 * d, 32), z)
    greet(sib, z)

    def scan(slot, found):
        i = ids[0, slot]
        hit = ids[1, slot] == z
        return tuple(jnp.where(hit & (i == coupled[a, r]), slot, found[a]) for a in range(4))

    found = lax.fori_loop(0, SLOTS, scan, (jnp.int32(-1),) * 4)
    pl.semaphore_wait(barrier, 23)

    @pl.when(z < 4)
    def _():
        load.wait()
        for a in range(4):
            block = vbuf[jnp.maximum(found[a], 0)]
            left[z, a] = jnp.where(found[a] >= 0, block, 0.0)

    def copy(src, dst, ssem, rsem, row, col):
        return pltpu.make_async_remote_copy(
            src_ref=src, dst_ref=dst, send_sem=ssem, recv_sem=rsem,
            device_id={"row": row, "col": col}, device_id_type=MESH,
        )

    sends = []

    def send(cond, *descs):
        @pl.when(cond)
        def _():
            for desc in descs:
                desc.start()

        sends.append((cond, descs))

    def post(cond, arrived, descs):
        @pl.when(cond)
        def _():
            for desc in arrived:
                desc.wait_recv()
            for desc in descs:
                desc.start()


    def travellers(d):
        if d == 0:
            return [(jnp.minimum(z, 3), z < 4, true, true)]
        ku = lax.rem(z + 8 - d, 8)
        reach = jnp.where(ku >= 2, 5, 2)
        kd = lax.rem(z + d, 8)
        depth = jnp.where(kd >= 2, 2, 5)
        return [
            (jnp.minimum(ku, 3), (ku <= 3) & (d <= reach), d < reach, None),
            (jnp.minimum(kd, 3), (kd <= 3) & (d <= depth), None, d < depth),
        ]

    def spread(k, q):
        block = right.at[y, k, 2 * h + q]
        return [copy(block, block, ys.at[k, n, q], yr.at[y, k, q], yo[n], z) for n in range(2)] + [
            copy(block, block, ss.at[y, k, q], sr.at[y, k, q], sib, z)
        ]

    def spread_x(k, q):
        block = right.at[y, k, 2 * h + q]
        return [copy(block, block, xs.at[k, n, q], xr.at[k, q], xo[n], z) for n in range(3)]

    def to_sibling(k, q):
        a = 2 - 2 * h + q
        return copy(left.at[k, a], right.at[y, k, a], os_.at[k, q], xr.at[k, q], sib, z)

    def z_event(d):
        group = travellers(d)
        for a in range(4):
            for k, valid, go_up, go_down in group:
                block = left.at[k, a]
                rise = copy(block, block, zus.at[k, a], zr.at[k, a], r, up)
                sink = copy(block, block, zds.at[k, a], zr.at[k, a], r, down)
                if d == 0:
                    post(valid, [], [rise, sink])
                elif go_up is not None:
                    post(valid, [rise], [])
                    post(valid & go_up, [], [rise])
                else:
                    post(valid, [sink], [])
                    post(valid & go_down, [], [sink])
                q = a % 2
                post(valid & source & (h != a // 2), [], [to_sibling(k, q)])

                @pl.when(valid & source & (h == a // 2))
                def _():
                    right[y, k, a] = left[k, a]
                    for desc in spread_x(k, q) + spread(k, q):
                        desc.start()

    def x_event(d):
        for k, valid, _, _ in travellers(d):
            mine = valid & jnp.logical_not(source)
            for q in range(2):
                block = right.at[y, k, 2 * h + q]
                post(mine, [copy(block, block, os_.at[k, q], xr.at[k, q], sib, z)], [])
                post(mine & origin, [], spread_x(k, q))
                post(mine, [], spread(k, q))

    def y_event(d, n):
        yy = lax.rem(y + (1, 3, 2)[n], 4)
        for k, valid, _, _ in travellers(d):
            part = lambda q: right.at[yy, k, 2 * h + q]
            on = lambda q, to: copy(part(q), part(q), yfs.at[k, q], yfr.at[k, q], to, z)
            share = lambda q: copy(part(q), part(q), ss.at[yy, k, q], sr.at[yy, k, q], sib, z)
            for q in (1 - n, n) if n < 2 else (0, 1):
                if n == 2:
                    post(valid, [on(q, yo[q])], [share(q)])
                else:
                    come = copy(part(q), part(q), ys.at[k, n, q], yr.at[yy, k, q], yo[n], z)
                    post(valid, [come], ([on(q, yo[1 - n])] if q == 1 - n else []) + [share(q)])

    first = lead.at[0, 4]

    def first_z():
        mine = (r == 0) & (z == 0)

        @pl.when(mine)
        def _():
            lead[0, 4] = left[0, 0]

        send(mine, *[copy(first, first, f1s.at[d - 1], fr, r, lax.rem(z + d, 8)) for d in range(1, 8)])

    def first_out(mine):
        send(
            mine,
            *[copy(first, first, f3s.at[n], fr, xo[n], z) for n in range(3)],
            copy(first, first, f4s, fr, sib, z),
        )

    def first_y():
        mine = r == 0
        pl.when(mine & (z != 0))(copy(first, first, f4s, fr, sib, z).wait_recv)
        send(mine, *[copy(first, first, f2s.at[n], fr, yo[n], z) for n in range(3)])
        first_out(mine)

    def first_x():
        mine = (h == 0) & (x == 0) & (y > 0)
        pl.when(mine)(copy(first, first, f4s, fr, sib, z).wait_recv)
        first_out(mine)

    def first_s():
        mine = (h == 0) & (x > 0)
        pl.when(mine)(copy(first, first, f4s, fr, sib, z).wait_recv)
        send(mine, copy(first, first, f4s, fr, sib, z))

    rows = lambda yy, xx: pl.ds(pl.multiple_of(32 * yy + 8 * xx, 8), 8)
    mine8 = rows(y, x)
    zc = jnp.minimum(z, 3)

    def here(j, k):
        i = 2 * j + h
        return (i >= k) & (i > 0)

    def slot_of(j, k):
        return k if j else 4 + jnp.minimum(k, 1)

    def lead_scatter():
        for j in range(2):
            mine = (r == 2 * j + h) & (z < 4) & here(j, z)
            slot = slot_of(j, zc)

            @pl.when(mine)
            def _():
                lead[h, slot, mine8] = left[zc, 0, mine8]

            descs = []
            for d in range(1, 16):
                p = lax.rem(y * 4 + x + d, 16)
                at = rows(p // 4, lax.rem(p, 4))
                part, target = left.at[zc, 0, at], lead.at[h, slot, at]
                descs.append(copy(part, target, g0s.at[d - 1], g0r.at[j], p * 2 + h, z))
            send(mine, *descs)

    def lead_planes():
        @pl.when(h == 0)
        def _():
            lead[0, 5, mine8] = jnp.zeros((8, B), F32)
            lead[0, 3, mine8] = jnp.zeros((8, B), F32)

        for j in range(2):
            mine = (z < 4) & here(j, z)
            part = lead.at[h, slot_of(j, zc), mine8]
            pl.when(mine & (r != 2 * j + h))(copy(part, part, g0s.at[0], g0r.at[j], sib, z).wait_recv)
            send(
                mine,
                *[
                    copy(part, part, g1s.at[j, d - 1], g1r.at[j, zc], r, lax.rem(z + d, 8))
                    for d in range(1, 8)
                ],
            )

    def lead_x():
        for j in range(2):
            for k in range(4 if j else 2):
                part = lead.at[h, slot_of(j, k), mine8]
                pl.when(here(j, k) & (z != k))(copy(part, part, g1s.at[j, 0], g1r.at[j, k], r, up).wait_recv)
        for first_slot, count in ((0, 4), (4, 2)):
            q = first_slot // 4
            part = lead.at[h, pl.ds(first_slot, count), mine8]
            send(
                (h == 1) | (q == 0),
                *[copy(part, part, g2s.at[q, n], g2r.at[q, x], xo[n], z) for n in range(3)],
            )

    def lead_y():
        for first_slot, count in ((0, 4), (4, 2)):
            q = first_slot // 4
            for d in (1, 3, 2):
                xx = lax.rem(x + d, 4)
                part = lead.at[h, pl.ds(first_slot, count), rows(y, xx)]
                pl.when((h == 1) | (q == 0))(copy(part, part, g2s.at[q, 0], g2r.at[q, xx], sib, z).wait_recv)
            part = lead.at[h, pl.ds(first_slot, count), pl.ds(pl.multiple_of(32 * y, 32), 32)]
            send(
                (h == 1) | (q == 0),
                *[copy(part, part, g3s.at[q, n], g3r.at[q, y], yo[n], z) for n in range(3)],
            )

    def lead_s():
        for first_slot, count in ((0, 4), (4, 2)):
            q = first_slot // 4
            for d in (1, 3, 2):
                yy = lax.rem(y + d, 4)
                part = lead.at[h, pl.ds(first_slot, count), pl.ds(pl.multiple_of(32 * yy, 32), 32)]
                pl.when((h == 1) | (q == 0))(copy(part, part, g3s.at[q, 0], g3r.at[q, yy], sib, z).wait_recv)
            part = lead.at[h, pl.ds(first_slot, count)]
            send((h == 1) | (q == 0), copy(part, part, g4s.at[q], g4r.at[q], sib, z))

    def lead_arrived(i):
        if i == 0:
            pl.when(h == 1)(copy(first, first, f4s, fr, sib, z).wait_recv)
        if i == 1:
            part = lead.at[1 - h, pl.ds(0, 4)]
            copy(part, part, g4s.at[0], g4r.at[0], sib, z).wait_recv()
            part = lead.at[1 - h, pl.ds(4, 2)]
            pl.when(h == 0)(copy(part, part, g4s.at[1], g4r.at[1], sib, z).wait_recv)

    steps = factor_lead(lead, m2, s, inverse, diag, lead_arrived)

    def work(count):
        for _ in range(count):
            next(steps, None)

    first_z()
    lead_scatter()
    z_event(0)
    lead_planes()
    z_event(1)
    first_y()
    x_event(0)
    z_event(2)
    first_x()
    lead_x()
    x_event(1)
    for n in range(2):
        y_event(0, n)
    z_event(3)
    first_s()
    lead_y()
    work(4)
    x_event(2)
    for n in range(2):
        work(4)
        y_event(1, n)
    work(4)
    y_event(0, 2)
    lead_s()
    z_event(4)
    work(6)
    x_event(3)
    for n in range(2):
        work(6)
        y_event(2, n)
    work(6)
    y_event(1, 2)
    z_event(5)
    work(6)
    x_event(4)
    for n in range(2):
        work(6)
        y_event(3, n)
    work(6)
    y_event(2, 2)
    x_event(5)
    for n in range(2):
        work(6)
        y_event(4, n)
    work(6)
    y_event(3, 2)
    for n in range(2):
        y_event(5, n)
    work(6)
    y_event(4, 2)
    y_event(5, 2)
    for _ in steps:
        pass

    for yy in range(4):
        for k in range(4):
            for q in range(2):
                block = right.at[yy, k, 2 - 2 * h + q]
                copy(block, block, ss.at[yy, k, q], sr.at[yy, k, q], sib, z).wait_recv()
    for cond, descs in sends:

        @pl.when(cond)
        def _():
            for desc in descs:
                desc.wait_send()

    for k in range(4):

        @pl.when(lax.rem(z + 8 - k, 8) < (5 if k >= 2 else 2))
        def _():
            for a in range(4):
                block = left.at[k, a]
                copy(block, block, zus.at[k, a], zr.at[k, a], r, up).wait_send()

        @pl.when(lax.rem(k + 8 - z, 8) < (2 if k >= 2 else 5))
        def _():
            for a in range(4):
                block = left.at[k, a]
                copy(block, block, zds.at[k, a], zr.at[k, a], r, down).wait_send()

        for q in range(2):
            pl.when(source)(to_sibling(k, q).wait_send)

            @pl.when(origin)
            def _():
                for desc in spread_x(k, q):
                    desc.wait_send()

            for desc in spread(k, q):
                desc.wait_send()
            part = right.at[y, k, q]
            copy(part, part, yfs.at[k, q], yfr.at[k, q], yo[q], z).wait_send()
            for n in range(3):
                yy = lax.rem(y + (1, 3, 2)[n], 4)
                block = right.at[yy, k, 2 * h + q]
                copy(block, block, ss.at[yy, k, q], sr.at[yy, k, q], sib, z).wait_send()


def exchange(ids, coupled, values):
    dma = pltpu.SemaphoreType.DMA
    vmem = pl.BlockSpec(memory_space=pltpu.VMEM)
    return pl.pallas_call(
        exchange_kernel,
        out_shape=(
            jax.ShapeDtypeStruct((4, 4, B, B), F32),
            jax.ShapeDtypeStruct((4, 4, 4, B, B), F32),
            jax.ShapeDtypeStruct((512, 512), F32),
            jax.ShapeDtypeStruct((4, B, B), F32),
        ),
        in_specs=[
            pl.BlockSpec(memory_space=pltpu.SMEM),
            pl.BlockSpec(memory_space=pltpu.SMEM),
            pl.BlockSpec(memory_space=pltpu.HBM),
        ],
        out_specs=(vmem, vmem, vmem, vmem),
        scratch_shapes=[
            pltpu.VMEM((SLOTS, B, B), F32),
            pltpu.VMEM((2, 6, B, B), F32),
            pltpu.VMEM((B, 2 * B), F32),
            pltpu.VMEM((512, 512), F32),
            dma,
            dma((4, 4)), dma((4, 4)), dma((4, 4)),
            dma((4, 3, 2)), dma((4, 2)), dma((4, 2)),
            dma((4, 2, 2)), dma((4, 4, 2)), dma((4, 2)), dma((4, 2)),
            dma((4, 4, 2)), dma((4, 4, 2)),
            dma, dma((7,)), dma((3,)), dma((3,)), dma,
            dma((15,)), dma((2,)),
            dma((2, 7)), dma((2, 4)),
            dma((2, 3)), dma((2, 4)),
            dma((2, 3)), dma((2, 4)),
            dma((2,)), dma((2,)),
        ],
        compiler_params=pltpu.CompilerParams(
            collective_id=0, has_side_effects=True, vmem_limit_bytes=46 << 20
        ),
        name="exchange",
    )(ids, coupled, values)


def eliminate(m2):
    sub = lax.broadcasted_iota(jnp.int32, (8, B), 0)
    nt = NB // 8
    for p in range(B // NB):
        b = NB * p
        for u in range(nt):
            cb = b + 8 * u
            T = {
                (i, t): m2[b + 8 * i : b + 8 * i + 8, B * t : B * t + B] for t in range(2) for i in range(u, nt)
            }
            C = {
                (i, j): jnp.broadcast_to(T[i, 0][:, cb + j : cb + j + 1], (8, B))
                for i in range(u, nt)
                for j in range(8)
            }
            sc = jnp.ones((8, B), F32)
            for j in range(8):
                piv = jnp.broadcast_to(C[u, j][j : j + 1, :], (8, B))
                inv = 1.0 / piv
                sc = jnp.where(sub == j, lax.rsqrt(piv), sc)
                rows = [jnp.broadcast_to(T[u, t][j : j + 1, :], (8, B)) for t in range(2)]
                cs = {jj: jnp.broadcast_to(C[u, jj][j : j + 1, :], (8, B)) for jj in range(j + 1, 8)}
                for i in range(u, nt):
                    m = C[i, j] * inv
                    if i == u:
                        if j == 7:
                            continue
                        m = jnp.where(sub > j, m, 0.0)
                    for jj in range(j + 1, 8):
                        C[i, jj] = C[i, jj] - m * cs[jj]
                    for t in range(2):
                        T[i, t] = T[i, t] - m * rows[t]
            for t in range(2):
                T[u, t] = T[u, t] * sc
            for (i, t), v in T.items():
                m2[b + 8 * i : b + 8 * i + 8, B * t : B * t + B] = v
            yield
        if b + NB < B:
            R = m2[b : b + NB, :]
            g = lax.dot_general(
                R[:, b + NB : B], R, (((0,), (0,)), ((), ())), precision=HIGH, preferred_element_type=F32
            )
            m2[b + NB : B, :] = m2[b + NB : B, :] - g
            yield


def factor_lead(lead, m2, s, e, diag, arrived):
    n = 4
    ri = lax.broadcasted_iota(jnp.int32, (B, B), 0)
    ci = lax.broadcasted_iota(jnp.int32, (B, B), 1)
    e[...] = jnp.zeros_like(e)
    for k in range(n):
        a, z = B * k, B * k + B
        if k == 0:
            arrived(0)
            m2[:, :B] = lead[0, 4]
        else:
            m2[:, :B] = s[a:z, a:z]
        m2[:, B:] = jnp.where(ri == ci, 1.0, 0.0).astype(F32)
        yield from eliminate(m2)
        if k == 0:
            for i in range(1, n):
                arrived(i)
                base = 4 if i < 2 else 0
                s[B * i : B * i + B, B * i : B * i + B] = lead[i % 2, base + i]
                for kk in range(i):
                    s[B * kk : B * kk + B, B * i : B * i + B] = lead[i % 2, base + kk].T
            yield
        li = jnp.where(ri >= ci, m2[:, B:], 0.0)
        diag[k] = jnp.where(ri >= ci, m2[:, :B].T, 0.0)
        parts = []
        if k < n - 1:
            parts.append(s[a:z, z:])
        if k > 0:
            parts.append(e[a:z, :a])
        R = jnp.dot(li, jnp.concatenate(parts, axis=1), precision=HIGH, preferred_element_type=F32)
        w = (n - 1 - k) * B
        if k > 0:
            e[a:z, :a] = R[:, w:]
        e[a:z, a:z] = li
        if k < n - 1:
            s[a:z, z:] = R[:, :w]
            yield
            full = jnp.concatenate([s[a:z, z:], e[a:z, :z]], axis=1)
            g = lax.dot_general(
                full[:, :w], full, (((0,), (0,)), ((), ())), precision=HIGH, preferred_element_type=F32
            )
            s[z:, z:] = s[z:, z:] - g[:, :w]
            e[z:, :z] = e[z:, :z] - g[:, w:]
        yield


def split(v):
    hi = v.astype(BF16)
    return hi, (v - hi.astype(F32)).astype(BF16)


def dot_nt(a, b):
    (ah, al), (bh, bl) = a, b
    return lax.dot_general(
        jnp.concatenate([ah, al, ah], axis=1),
        jnp.concatenate([bh, bh, bl], axis=1),
        (((1,), (1,)), ((), ())),
        preferred_element_type=F32,
    )


def finish_kernel(
    ids, coupled, values, left, right, inverse, diag, out,
    obuf, ehi, elo, whi, wlo, g, osem,
):
    r = lax.axis_index("row")
    hi, lo = split(inverse[...])
    ehi[...] = hi
    elo[...] = lo

    def factor_rows(blocks):
        cat = [blocks[k].reshape(4 * B, B) for k in range(4)]
        parts = [split(c) for c in cat]
        xh = jnp.concatenate([p[0] for p in parts], axis=1)
        xl = jnp.concatenate([p[1] for p in parts], axis=1)
        h = 2 * B
        w0 = dot_nt((xh[:, :h], xl[:, :h]), (ehi[:h, :h], elo[:h, :h]))
        w1 = dot_nt((xh, xl), (ehi[h:, :], elo[h:, :]))
        return jnp.concatenate([w0, w1], axis=1)

    wl = factor_rows(left)
    for n in range(4):
        for a in range(4):
            g[64 + 4 * n + a] = -wl[B * a : B * a + B, B * n : B * n + B]
    g[80] = jnp.zeros((B, B), F32)

    @pl.when(r < 4)
    def _():
        g[64 + 4 * r] = -diag[r]

    hi, lo = split(wl)
    whi[...] = hi
    wlo[...] = lo

    @pl.loop(0, 4)
    def _(y):
        wr = factor_rows(right.at[y])
        wrh, wrl = split(wr)
        for c in range(2):
            p = dot_nt((whi[...], wlo[...]), (wrh[256 * c : 256 * c + 256], wrl[256 * c : 256 * c + 256]))
            for b in range(2):
                for a in range(4):
                    g[(y * 4 + 2 * c + b) * 4 + a] = p[B * a : B * a + B, B * b : B * b + B]

    @pl.loop(0, SLOTS, unroll=4)
    def _(slot):
        i = ids[0, slot]
        j = ids[1, slot]
        a = jnp.int32(0)
        own = jnp.int32(0)
        b = jnp.int32(0)
        r2 = j & 31
        for n in range(4):
            hit = i == coupled[n, r]
            a = jnp.where(hit, n, a)
            own = jnp.where(hit, 1, own)
            b = jnp.where(j == coupled[n, r2], n, b)
        found = own == 1
        trailing = found & (j >= 4)
        panel = found & (j < 4)
        place = jnp.where(trailing, ((r2 // 8) * 4 + b) * 4 + a, jnp.where(panel, 64 + 4 * j + a, 80))
        keep = (i >= 0) & jnp.logical_not(panel)
        obuf[slot] = jnp.where(keep, values[slot], 0.0) - g[place]
        pltpu.make_async_copy(obuf.at[slot], out.at[slot], osem).start()

    pltpu.make_async_copy(obuf, out, osem).wait()


def finish(ids, coupled, values, left, right, inverse, diag):
    smem = pl.BlockSpec(memory_space=pltpu.SMEM)
    vmem = pl.BlockSpec(memory_space=pltpu.VMEM)
    hbm = pl.BlockSpec(memory_space=pltpu.HBM)
    dma = pltpu.SemaphoreType.DMA
    return pl.pallas_call(
        finish_kernel,
        out_shape=jax.ShapeDtypeStruct((SLOTS, B, B), F32),
        in_specs=[smem, smem, vmem, vmem, vmem, vmem, vmem],
        out_specs=hbm,
        scratch_shapes=[
            pltpu.VMEM((SLOTS, B, B), F32),
            pltpu.VMEM((512, 512), BF16),
            pltpu.VMEM((512, 512), BF16),
            pltpu.VMEM((512, 512), BF16),
            pltpu.VMEM((512, 512), BF16),
            pltpu.VMEM((81, B, B), F32),
            dma,
        ],
        compiler_params=pltpu.CompilerParams(vmem_limit_bytes=32 << 20),
        name="finish",
    )(ids, coupled, values, left, right, inverse, diag)


def body(values, block_ids, coupled_rows):
    ids = block_ids[0, 0].T
    coupled = coupled_rows.T
    left, right, inverse, diag = exchange(ids, coupled, values[0, 0])
    out = finish(ids, coupled, values[0, 0], left, right, inverse, diag)
    return out[None, None]


def solution(mesh):
    placed = (P("row", "col", None, None, None), P("row", "col", None, None), P())
    return jax.shard_map(
        body,
        mesh=mesh,
        in_specs=placed,
        out_specs=P("row", "col", None, None, None),
        check_vma=False,
    )
```
